768 devices in a mesh: group: 96 (over x, z, core), sub: 8 (over y).
Axes of the slice: x: 4, y: 8, z: 12, core: 2. Of those that a mesh axis runs over, the one named last changes fastest.
Arguments:
- fields: float32 [4, 84, 98304], P(None, None, ('group', 'sub')), may hold values from -6 to 6
- diff_ops: float32 [3, 84, 84], replicated, may hold values from -0.625 to 0.625
- face_interp: float32 [112, 84], replicated, may hold values from -0.625 to 0.625
- lift: float32 [84, 112], replicated, may hold values from -0.5 to 0.5
- inv_jacobian: float32 [3, 3, 98304], P(None, None, ('group', 'sub')), may hold values from -4 to 4
- face_scale: float32 [4, 98304], P(None, ('group', 'sub')), may hold values from 1 to 4
- normal_angle: float32 [2, 4, 98304], P(None, None, ('group', 'sub')), may hold values from -3.140625 to 3.140625
- reflect: float32 [4], replicated, may hold values from -0.5 to 1
- send_list: int32 [4, 12288], P(None, ('group', 'sub')), may hold values from 0 to 511, as said below
- recv_map: int32 [4, 98304], P(None, ('group', 'sub')), may hold values from 0 to 575, as said below
- face_class: int32 [4, 98304], P(None, ('group', 'sub')), may hold values from 0 to 4
Outputs:
- pressure_velocity: float32 [4, 84, 98304], P(None, None, ('group', 'sub'))
The draws below stay inside these ranges and needn't reach their ends.
Inputs may be any that keep to these rules, and one draw needn't show every extreme that they name: `recv_map`: values below 512 name a local face of the same device; 512 + j * 16 + s names slot s of the buffer received from neighbour j (0 previous sub, 1 next sub, 2 previous group, 3 next group). Only read where face_class is 0; the used slots from each neighbour form a prefix, and no slot of a missing device is named. `send_list`: local face ids, distinct within a device.
All inputs are finite; a program needn't handle non-finite values.
Results may differ from the reference program's by a relative error of at most 0.0003.
Values sent between devices are 32-bit elements; how exact they have to be, the bound alone decides.
A program may use at most 32 MiB of HBM per device.

```python
import math
import jax
import jax.numpy as jnp
from jax import lax

NP = 84
NFP = 28
ELEM_DEV = 128
SECTIONS = 5
NCLASS = 4
CAP = 16
ELEMS = 98304
N_GROUP = 96
N_SUB = 8


def connect(key):
    device_count = N_GROUP * N_SUB
    face_total = 4 * ELEM_DEV
    key_sub, key_group, key_perm, key_class = jax.random.split(jax.random.fold_in(key, 11), 4)
    lowest = max(1, CAP // 2)
    link_sub = jax.random.randint(key_sub, (device_count,), lowest, CAP + 1).at[0].set(CAP)
    link_group = jax.random.randint(key_group, (device_count,), lowest, CAP + 1).at[0].set(CAP)
    device = jnp.arange(device_count, dtype=jnp.int32)
    column = device % N_SUB
    row_index = device // N_SUB
    link_sub = jnp.where(column < N_SUB - 1, link_sub, 0)
    link_group = jnp.where(row_index < N_GROUP - 1, link_group, 0)
    counts = jnp.stack([jnp.roll(link_sub, 1), link_sub, jnp.roll(link_group, N_SUB), link_group], axis=1)
    orders = jax.vmap(lambda one_key: jax.random.permutation(one_key, face_total))(jax.random.split(key_perm, device_count)).astype(jnp.int32)
    position = jnp.arange(face_total, dtype=jnp.int32)
    slot_dir = jnp.minimum(position // CAP, 3)
    slot_pos = position % CAP
    used = (position < 4 * CAP)[None, :] & (slot_pos[None, :] < counts[:, slot_dir])
    base = 4 * CAP + ELEM_DEV // 4
    local_face = position >= base
    partner = jnp.where(local_face, jnp.bitwise_xor(position - base, 1) + base, position)
    partner_face = jnp.take_along_axis(orders, jnp.broadcast_to(partner[None, :], orders.shape), axis=1)
    value_pos = jnp.where(used, 4 * ELEM_DEV + position[None, :], jnp.where(local_face[None, :], partner_face, orders))
    class_draw = jax.random.randint(key_class, (device_count, face_total), 1, NCLASS + 1)
    class_pos = jnp.where(used | local_face[None, :], 0, class_draw)
    place = jax.vmap(lambda order, value: jnp.zeros((face_total,), jnp.int32).at[order].set(value))
    recv_faces = place(orders, value_pos.astype(jnp.int32))
    class_faces = place(orders, class_pos.astype(jnp.int32))
    sends = orders[:, :4 * CAP].reshape(device_count, 4, CAP)
    sends = jnp.stack([sends[:, 1], sends[:, 0], sends[:, 3], sends[:, 2]], axis=1)
    send_whole = sends.transpose(1, 0, 2).reshape(4, device_count * CAP)
    recv_whole = recv_faces.reshape(device_count, 4, ELEM_DEV).transpose(1, 0, 2).reshape(4, device_count * ELEM_DEV)
    class_whole = class_faces.reshape(device_count, 4, ELEM_DEV).transpose(1, 0, 2).reshape(4, device_count * ELEM_DEV)
    return (send_whole, recv_whole, class_whole)


def draw_send_list(key, part):
    return connect(key)[0]


def draw_recv_map(key, part):
    return connect(key)[1]


def draw_face_class(key, part):
    return connect(key)[2]


def steps_of(own_key, dims, cuts, low, top_value):
    loudness = 1.0
    for dim, shards_of in cuts:
        draws = jax.random.uniform(jax.random.fold_in(jax.random.fold_in(own_key, 6), dim), (shards_of,), jnp.float32, low / len(cuts), top_value / len(cuts))
        loudness = loudness * jnp.repeat(jnp.exp(draws), dims[dim] // shards_of).reshape((-1,) + (1,) * (len(dims) - 1 - dim))
    return loudness


def scatter_about(stream_key, shape, scale, reach, pieces=(), kind=jnp.bfloat16):
    factor_of = steps_of(stream_key, shape, pieces, -0.22, 0.18) if pieces else 1.0
    drawn = jax.random.normal(stream_key, shape, jnp.float32) * scale * factor_of
    return jnp.minimum(jnp.maximum(drawn, -reach), reach).astype(kind)


def setup_inputs(seed: int = 0) -> dict:
    arg_keys = jax.random.split(jax.random.key(seed), 12)
    fields = scatter_about(arg_keys[0], (4, NP, ELEMS), 1.0, 6.0, ((2, 768),), jnp.float32)
    diff_ops = scatter_about(arg_keys[1], (3, NP, NP), NP ** -0.5, 0.625, (), jnp.float32)
    face_interp = scatter_about(arg_keys[2], (4 * NFP, NP), NP ** -0.5, 0.625, (), jnp.float32)
    lift = scatter_about(arg_keys[3], (NP, 4 * NFP), (4 * NFP) ** -0.5, 0.5, (), jnp.float32)
    inv_jacobian = scatter_about(arg_keys[4], (3, 3, ELEMS), 1.0, 4.0, ((2, 768),), jnp.float32)
    face_scale = jnp.clip(jnp.exp(math.log(4.0) - 1.3862944 * jax.random.uniform(arg_keys[5], (4, ELEMS), jnp.float32) ** steps_of(arg_keys[5], (4, ELEMS), ((1, 768),), -0.2, 0.2)), 1.0, 4.0)
    normal_angle = jnp.clip(jax.random.uniform(arg_keys[6], (2, 4, ELEMS), jnp.float32, -3.140625, 3.140625), -3.140625, 3.140625)
    reflect = jnp.clip(jax.random.uniform(arg_keys[7], (NCLASS,), jnp.float32, -0.5, 1.0), -0.5, 1.0)
    send_list = draw_send_list(jax.random.fold_in(arg_keys[11], 71), 0)
    recv_map = draw_recv_map(jax.random.fold_in(arg_keys[11], 71), 0)
    face_class = draw_face_class(jax.random.fold_in(arg_keys[11], 71), 0)
    return {"fields": fields, "diff_ops": diff_ops, "face_interp": face_interp, "lift": lift, "inv_jacobian": inv_jacobian, "face_scale": face_scale, "normal_angle": normal_angle, "reflect": reflect, "send_list": send_list, "recv_map": recv_map, "face_class": face_class}


RK_A = (0.0, -567301805773.0 / 1357537059087.0, -2404267990393.0 / 2016746695238.0, -3550918686646.0 / 2091501179385.0, -1275806237668.0 / 842570457699.0)
RK_B = (1432997174477.0 / 9575080441755.0, 5161836677717.0 / 13612068292357.0, 1720146321549.0 / 2090206949498.0, 3134564353537.0 / 4481467310338.0, 2277821191437.0 / 14882151754819.0)
DT = 0.3
HIGH = lax.Precision.HIGHEST


def face_traces(state_now, face_interp, face_count):
    traces = jnp.einsum('jn,fne->fje', face_interp, state_now, precision=HIGH)
    nfield, trace_rows, elem_count = traces.shape
    per_face = traces.reshape(nfield, face_count, trace_rows // face_count, elem_count).transpose(0, 2, 1, 3)
    return per_face.reshape(nfield, trace_rows // face_count, face_count * elem_count)


def unit_normals(angles):
    first, second = angles[0], angles[1]
    return jnp.stack([jnp.cos(first) * jnp.cos(second), jnp.sin(first) * jnp.cos(second), jnp.sin(second)])


def face_reflect(face_class, reflect):
    classes = jnp.arange(1, reflect.shape[0] + 1, dtype=jnp.int32)
    return jnp.sum(jnp.where(face_class[None] == classes[:, None, None], reflect[:, None, None], 0.0), axis=0)


def tendency(state_now, own_trace, neighbour, diff_ops, lift, inv_jacobian, face_scale, normal_dirs, interior, reflect_face):
    face_count = face_scale.shape[0]
    elem_count = state_now.shape[2]
    normal_rows = normal_dirs.reshape(3, 1, -1)
    un_own = jnp.sum(normal_rows * own_trace[1:4], axis=0)
    un_nbr = jnp.sum(normal_rows * neighbour[1:4], axis=0)
    jump_term = 0.5 * ((neighbour[0] - un_nbr) - (own_trace[0] - un_own))
    wall_term = 0.5 * (reflect_face.reshape(1, -1) * (own_trace[0] + un_own) - (own_trace[0] - un_own))
    upwind = jnp.where(interior.reshape(1, -1), jump_term, wall_term) * face_scale.reshape(1, -1)
    flux_terms = jnp.concatenate([upwind[None], -normal_rows * upwind[None]], axis=0)
    face_rows = flux_terms.shape[1]
    flux_terms = flux_terms.reshape(4, face_rows, face_count, elem_count).transpose(0, 2, 1, 3).reshape(4, face_count * face_rows, elem_count)
    lifted = jnp.einsum('nj,fje->fne', lift, flux_terms, precision=HIGH)
    slopes = jnp.einsum('anm,fme->afne', diff_ops, state_now, precision=HIGH)
    grad_p = jnp.einsum('ace,ane->cne', inv_jacobian, slopes[:, 0], precision=HIGH)
    diverg = jnp.einsum('ace,acne->ne', inv_jacobian, slopes[:, 1:4], precision=HIGH)
    return jnp.concatenate([-diverg[None], -grad_p], axis=0) + lifted


def reference(fields, diff_ops, face_interp, lift, inv_jacobian, face_scale, normal_angle, reflect, send_list, recv_map, face_class):
    device_count = N_GROUP * N_SUB

    def split_dev(whole):
        leading = whole.shape[:-1]
        return jnp.moveaxis(whole.reshape(leading + (device_count, ELEM_DEV)), -2, 0)

    state_now = split_dev(fields)
    jacobian_dev = split_dev(inv_jacobian)
    scale_dev = split_dev(face_scale)
    angle_dev = split_dev(normal_angle)
    lookup_dev = split_dev(recv_map)
    class_dev = split_dev(face_class)
    sends = jnp.moveaxis(send_list.reshape(4, device_count, CAP), 1, 0)
    residue = jnp.zeros_like(state_now)

    def pack(item):
        own_trace = face_traces(item[0], face_interp, 4)
        return jnp.moveaxis(jnp.take(own_trace, item[1], axis=2), 2, 0)

    def local(item):
        state_one, got, jacobian_one, scale_one, angle_one, lookup_one, class_one = item
        own_trace = face_traces(state_one, face_interp, 4)
        source_table = jnp.concatenate([own_trace, got[0], got[1], got[2], got[3]], axis=2)
        neighbour = jnp.take(source_table, lookup_one.reshape(-1), axis=2)
        return tendency(state_one, own_trace, neighbour, diff_ops, lift, jacobian_one, scale_one,
                        unit_normals(angle_one).reshape(3, -1), (class_one == 0).reshape(-1),
                        face_reflect(class_one, reflect).reshape(-1))

    for section_index in range(SECTIONS):
        packed = lax.map(pack, (state_now, sends)).reshape(N_GROUP, N_SUB, 4, 4, NFP, CAP)
        empty_sub = jnp.zeros_like(packed[:, :1, 0])
        empty_group = jnp.zeros_like(packed[:1, :, 0])
        from_sub_left = jnp.concatenate([empty_sub, packed[:, :-1, 0]], axis=1)
        from_sub_right = jnp.concatenate([packed[:, 1:, 1], empty_sub], axis=1)
        from_group_left = jnp.concatenate([empty_group, packed[:-1, :, 2]], axis=0)
        from_group_right = jnp.concatenate([packed[1:, :, 3], empty_group], axis=0)
        arrived = jnp.stack([from_sub_left, from_sub_right, from_group_left, from_group_right], axis=2)
        arrived = arrived.reshape(device_count, 4, 4, NFP, CAP)
        change = lax.map(local, (state_now, arrived, jacobian_dev, scale_dev, angle_dev, lookup_dev, class_dev))
        residue = RK_A[section_index] * residue + DT * change
        state_now = state_now + RK_B[section_index] * residue
    return jnp.moveaxis(state_now, 0, -2).reshape(4, NP, ELEMS)
```

```python
import functools

import jax
import jax.numpy as jnp
from jax import lax
from jax.experimental import pallas as pl
from jax.experimental.pallas import tpu as pltpu
from jax.sharding import PartitionSpec as P

MESH = pl.DeviceIdType.MESH
F32 = jnp.float32
BF16 = jnp.bfloat16
RK_A = (
    0.0,
    -567301805773.0 / 1357537059087.0,
    -2404267990393.0 / 2016746695238.0,
    -3550918686646.0 / 2091501179385.0,
    -1275806237668.0 / 842570457699.0,
)
RK_B = (
    1432997174477.0 / 9575080441755.0,
    5161836677717.0 / 13612068292357.0,
    1720146321549.0 / 2090206949498.0,
    3134564353537.0 / 4481467310338.0,
    2277821191437.0 / 14882151754819.0,
)
DT = 0.3
SECTIONS = 5
NP = 84
NR = 88
FR = 32
NFP = 28
ELEM = 128
FACES = 4 * ELEM
CAP = 16
SLOTS = 4 * CAP
BODY = 80


def iota(shape, dim):
    return lax.broadcasted_iota(jnp.int32, shape, dim)


def ones_where(cond):
    return jnp.where(cond, 1.0, 0.0).astype(BF16)


def halves(x):
    high = x.astype(BF16)
    return high, (x - high.astype(F32)).astype(BF16)


def mm(a, b):
    return jnp.dot(a, b, preferred_element_type=F32)


def mm_nt(a, b):
    return lax.dot_general(a, b, (((1,), (1,)), ((), ())), preferred_element_type=F32)


def spread_nodes():
    r, j = iota((NP, 256), 0), iota((NP, 256), 1)
    body = r < BODY
    high = (body & ((j == r) | (j == r + BODY))) | (~body & ((j == r + 160) | (j == r + 164)))
    low = (body & (j == r + 2 * BODY)) | (~body & (j == r + 168))
    return ones_where(high), ones_where(low)


def stack_state(q_ref, st_ref):
    for f in range(4):
        cols = slice(f * ELEM, (f + 1) * ELEM)
        high, low = halves(q_ref[f, 0:BODY, :])
        st_ref[0:BODY, cols] = high
        st_ref[BODY : 2 * BODY, cols] = low
        st_ref[2 * BODY : 3 * BODY, cols] = high
        tail = q_ref[f, BODY:NR, :]
        tail_high = tail.astype(BF16).astype(F32)
        tail_low = pltpu.roll(tail - tail_high, 4, 0)
        st_ref[3 * BODY : 256, cols] = jnp.concatenate([tail_high + tail_low, tail_high], axis=0).astype(BF16)


def kernel(
    n_group,
    n_sub,
    fields_hbm,
    diff_hbm,
    interp_hbm,
    lift_hbm,
    jac_hbm,
    scale_hbm,
    angle_hbm,
    reflect_hbm,
    send_hbm,
    recv_hbm,
    class_hbm,
    out_ref,
    fields,
    diff,
    interp,
    lift,
    jac,
    scale,
    angle,
    reflect,
    send,
    recv,
    klass,
    q,
    res,
    st,
    fpad,
    w_face,
    w_diff,
    w_lift,
    sel,
    oh_local,
    oh_far,
    coef,
    jcoef,
    own,
    table,
    upl,
    flux,
    send_buf,
    recv_buf,
    load_sem,
    send_sem,
    recv_sem,
):
    g, s = lax.axis_index("group"), lax.axis_index("sub")
    g_next, g_prev = lax.rem(g + 1, n_group), lax.rem(g + n_group - 1, n_group)
    s_next, s_prev = lax.rem(s + 1, n_sub), lax.rem(s + n_sub - 1, n_sub)
    peers = ((g, s_next), (g, s_prev), (g_next, s), (g_prev, s))

    loads = [
        pltpu.make_async_copy(src, dst, load_sem.at[i])
        for i, (src, dst) in enumerate(
            (
                (interp_hbm, interp),
                (fields_hbm, fields),
                (send_hbm, send),
                (recv_hbm, recv),
                (class_hbm, klass),
                (angle_hbm, angle),
                (scale_hbm, scale),
                (reflect_hbm, reflect),
                (jac_hbm, jac),
                (diff_hbm, diff),
                (lift_hbm, lift),
            )
        )
    ]
    for load in loads:
        load.start()
    barrier = pltpu.get_barrier_semaphore()
    for peer in peers:
        pl.semaphore_signal(barrier, inc=1, device_id=peer, device_id_type=MESH)

    spread_high, spread_low = spread_nodes()
    fpad[...] = jnp.zeros_like(fpad)
    loads[0].wait()
    for k in range(4):
        fpad[k * FR : k * FR + NFP, :] = interp[k * NFP : (k + 1) * NFP, :]
    high, low = halves(fpad[...])
    w_face[...] = (mm(high, spread_high) + mm(low, spread_low)).astype(BF16)
    loads[1].wait()
    for f in range(4):
        q[f, BODY:NR, :] = jnp.zeros((NR - BODY, ELEM), F32)
        q[f, 0:NP, :] = fields[f]
    stack_state(q, st)
    loads[2].wait()
    for j in range(4):
        wanted = jnp.transpose(jnp.broadcast_to(send[j : j + 1, :], (CAP, CAP)), (1, 0))[:, 0:1]
        sel[j * CAP : (j + 1) * CAP, :] = ones_where(iota((CAP, FACES), 1) == wanted)

    def copy_to(m, j):
        return pltpu.make_async_remote_copy(
            src_ref=send_buf.at[m, j],
            dst_ref=recv_buf.at[m, j],
            send_sem=send_sem.at[m, j],
            recv_sem=recv_sem.at[m, j],
            device_id=peers[j],
            device_id_type=MESH,
        )

    def face_part(m):
        traces = mm(w_face[...], st[...])
        for f in range(4):
            for k in range(4):
                block = traces[k * FR : (k + 1) * FR, f * ELEM : (f + 1) * ELEM]
                own[f, k] = block
                high, low = halves(block)
                table[f * FR : (f + 1) * FR, k * ELEM : (k + 1) * ELEM] = high
                table[4 * FR + f * FR : 4 * FR + (f + 1) * FR, k * ELEM : (k + 1) * ELEM] = low
        packed = mm_nt(sel[...], table[...])
        packed = packed[:, 0:128] + packed[:, 128:256]
        for j in range(4):
            send_buf[m, j] = packed[j * CAP : (j + 1) * CAP, :]

    def launch(m):
        for j in (2, 3, 0, 1):
            copy_to(m, j).start()

    def c8(i, k):
        return coef[i, k][None]

    def tile(x):
        return x.reshape(FR // 8, 8, ELEM)

    def local_part(m, a_now):
        vol = None
        for a in range(3):
            slopes = mm(w_diff[a], st[:, ELEM : 4 * ELEM])
            for c in range(3):
                term = slopes[:, c * ELEM : (c + 1) * ELEM].reshape(NR // 8, 8, ELEM) * jcoef[a, c][None]
                vol = term if vol is None else vol + term
        res[0] = a_now * res[0] + vol.reshape(NR, ELEM)
        slopes = [mm(w_diff[a], st[:, 0:ELEM]).reshape(NR // 8, 8, ELEM) for a in range(3)]
        for c in range(3):
            vol = sum(slopes[a] * jcoef[a, c][None] for a in range(3))
            res[1 + c] = a_now * res[1 + c] + vol.reshape(NR, ELEM)
        near = mm(table[...], oh_local[...])
        near = near[0:128, :] + near[128:256, :]
        for k in range(4):
            po, uo, vo, wo = (tile(own[f, k]) for f in range(4))
            pn, un, vn, wn = (
                tile(near[f * FR : (f + 1) * FR, k * ELEM : (k + 1) * ELEM]) for f in range(4)
            )
            nx, ny, nz, sc, rf = (c8(i, k) for i in range(5))
            minus = nx * uo + ny * vo + nz * wo
            got = pn + (nx * un + ny * vn + nz * wn)
            up = sc * (got + rf * (po - minus) - (po + minus))
            upl[k] = up.reshape(FR, ELEM)

    def far_part(m, b_now, last):
        arrived = recv_buf[m].reshape(SLOTS, 128)
        high = arrived.astype(BF16).astype(F32)
        both = jnp.concatenate([high, arrived - high], axis=0)
        far = mm(jnp.transpose(both, (1, 0)).astype(BF16), oh_far[...])
        for k in range(4):
            pn, un, vn, wn = (
                tile(far[f * FR : (f + 1) * FR, k * ELEM : (k + 1) * ELEM]) for f in range(4)
            )
            nx, ny, nz, sc = (c8(i, k) for i in range(4))
            up = tile(upl[k]) + sc * (pn + (nx * un + ny * vn + nz * wn))
            for f, term in enumerate((up, nx * up, ny * up, nz * up)):
                high, low = halves(term.reshape(FR, ELEM))
                flux[k * FR : (k + 1) * FR, f * ELEM : (f + 1) * ELEM] = high
                flux[4 * FR + k * FR : 4 * FR + (k + 1) * FR, f * ELEM : (f + 1) * ELEM] = low
        lifted = mm(w_lift[...], flux[...])
        lifted = lifted[0:NR, :] + lifted[NR : 2 * NR, :]
        for f in range(4):
            change = res[f] + lifted[:, f * ELEM : (f + 1) * ELEM]
            new = q[f] + b_now * change
            res[f] = change
            q[f] = new

    face_part(0)
    pl.semaphore_wait(barrier, 4)
    launch(0)

    for load in loads[3:]:
        load.wait()
    for k in range(4):
        rows = slice(k * ELEM, (k + 1) * ELEM)
        where = jnp.where(klass[k : k + 1, :] == 0, recv[k : k + 1, :], -1)
        oh_local[:, rows] = ones_where(iota((FACES, ELEM), 0) == where)
        slot = iota((2 * SLOTS, ELEM), 0)
        slot = jnp.where(slot >= SLOTS, slot - SLOTS, slot)
        oh_far[:, rows] = ones_where(slot + FACES == where)
        first, second = angle[0, k : k + 1, :], angle[1, k : k + 1, :]
        flat = jnp.cos(second)
        kinds = klass[k : k + 1, :]
        mirror = jnp.zeros((1, ELEM), F32)
        for c in range(4):
            mirror = mirror + jnp.where(kinds == c + 1, reflect[c], 0.0)
        for i, row in enumerate(
            (
                -(jnp.cos(first) * flat),
                -(jnp.sin(first) * flat),
                -jnp.sin(second),
                0.5 * scale[k : k + 1, :],
                mirror,
            )
        ):
            coef[i, k] = jnp.broadcast_to(row, (8, ELEM))
    for a in range(3):
        high, low = halves(diff[a] * (-DT))
        w_diff[a] = jnp.zeros((NR, 256), BF16)
        w_diff[a, 0:NP, :] = (mm(high, spread_high) + mm(low, spread_low)).astype(BF16)
        for c in range(3):
            jcoef[a, c] = jnp.broadcast_to(jac[a, c : c + 1, :], (8, ELEM))
    r, j = iota((4 * NFP, 4 * FR), 0), iota((4 * NFP, 4 * FR), 1)
    face = (r >= NFP).astype(jnp.int32) + (r >= 2 * NFP).astype(jnp.int32) + (r >= 3 * NFP).astype(jnp.int32)
    spread_face = ones_where(j == r + (FR - NFP) * face)
    high, low = halves(lift[...] * DT)
    high, low = mm(high, spread_face).astype(BF16), mm(low, spread_face).astype(BF16)
    w_lift[...] = jnp.zeros_like(w_lift)
    w_lift[0:NP, 0:128] = high
    w_lift[0:NP, 128:256] = high
    w_lift[NR : NR + NP, 0:128] = low
    for f in range(4):
        res[f] = jnp.zeros((NR, ELEM), F32)

    def finish(m, b_now):
        for j in range(4):
            copy_to(m, j).wait_recv()
        far_part(m, b_now, False)
        for j in range(4):
            copy_to(m, j).wait_send()

    def pick(values, m):
        out = jnp.float32(values[0])
        for i in range(1, SECTIONS):
            out = jnp.where(m == i, jnp.float32(values[i]), out)
        return out

    def section(m, carry):
        local_part(m - 1, pick(RK_A, m - 1))
        finish(m - 1, pick(RK_B, m - 1))
        stack_state(q, st)
        face_part(m)
        launch(m)
        return carry

    lax.fori_loop(1, SECTIONS, section, 0)
    local_part(SECTIONS - 1, RK_A[-1])
    finish(SECTIONS - 1, RK_B[-1])
    for f in range(4):
        out_ref[f] = q[f, 0:NP, :]


def shards(n_group, n_sub, *args):
    shapes = [a.shape for a in args]
    vm = pltpu.VMEM
    loaded = [
        pltpu.SMEM(x.shape, x.dtype) if i == 7 else vm(x.shape, x.dtype) for i, x in enumerate(args)
    ]
    return pl.pallas_call(
        functools.partial(kernel, n_group, n_sub),
        out_shape=jax.ShapeDtypeStruct(shapes[0], F32),
        in_specs=[pl.BlockSpec(memory_space=pl.ANY)] * len(args),
        out_specs=pl.BlockSpec(memory_space=pltpu.VMEM),
        scratch_shapes=loaded
        + [
            vm((4, NR, ELEM), F32),
            vm((4, NR, ELEM), F32),
            vm((256, FACES), BF16),
            vm((4 * FR, NP), F32),
            vm((4 * FR, 256), BF16),
            vm((3, NR, 256), BF16),
            vm((2 * NR, 256), BF16),
            vm((SLOTS, FACES), BF16),
            vm((FACES, FACES), BF16),
            vm((2 * SLOTS, FACES), BF16),
            vm((5, 4, 8, ELEM), F32),
            vm((3, 3, 8, ELEM), F32),
            vm((4, 4, FR, ELEM), F32),
            vm((256, FACES), BF16),
            vm((4, FR, ELEM), F32),
            vm((256, FACES), BF16),
            vm((SECTIONS, 4, CAP, 128), F32),
            vm((SECTIONS, 4, CAP, 128), F32),
            pltpu.SemaphoreType.DMA((len(args),)),
            pltpu.SemaphoreType.DMA((SECTIONS, 4)),
            pltpu.SemaphoreType.DMA((SECTIONS, 4)),
        ],
        compiler_params=pltpu.CompilerParams(collective_id=0, has_side_effects=True),
        name="sections",
    )(*args)


def solution(mesh):
    both = ("group", "sub")
    return jax.shard_map(
        functools.partial(shards, mesh.shape["group"], mesh.shape["sub"]),
        mesh=mesh,
        in_specs=(
            P(None, None, both),
            P(),
            P(),
            P(),
            P(None, None, both),
            P(None, both),
            P(None, None, both),
            P(),
            P(None, both),
            P(None, both),
            P(None, both),
        ),
        out_specs=P(None, None, both),
        check_vma=False,
    )
```

```python
import functools

import jax
import jax.numpy as jnp
from jax import lax
from jax.experimental import pallas as pl
from jax.experimental.pallas import tpu as pltpu
from jax.sharding import PartitionSpec as P

MESH = pl.DeviceIdType.MESH
F32 = jnp.float32
BF16 = jnp.bfloat16
RK_A = (
    0.0,
    -567301805773.0 / 1357537059087.0,
    -2404267990393.0 / 2016746695238.0,
    -3550918686646.0 / 2091501179385.0,
    -1275806237668.0 / 842570457699.0,
)
RK_B = (
    1432997174477.0 / 9575080441755.0,
    5161836677717.0 / 13612068292357.0,
    1720146321549.0 / 2090206949498.0,
    3134564353537.0 / 4481467310338.0,
    2277821191437.0 / 14882151754819.0,
)
DT = 0.3
SECTIONS = 5
NP = 84
NR = 88
FR = 32
NFP = 28
ELEM = 128
FACES = 4 * ELEM
CAP = 16
SLOTS = 4 * CAP
BODY = 80


def iota(shape, dim):
    return lax.broadcasted_iota(jnp.int32, shape, dim)


def ones_where(cond):
    return jnp.where(cond, 1.0, 0.0).astype(BF16)


def halves(x):
    high = x.astype(BF16)
    return high, (x - high.astype(F32)).astype(BF16)


def mm(a, b):
    return jnp.dot(a, b, preferred_element_type=F32)


def mm_nt(a, b):
    return lax.dot_general(a, b, (((1,), (1,)), ((), ())), preferred_element_type=F32)


def spread_nodes():
    r, j = iota((NP, 256), 0), iota((NP, 256), 1)
    body = r < BODY
    high = (body & ((j == r) | (j == r + BODY))) | (~body & ((j == r + 160) | (j == r + 164)))
    low = (body & (j == r + 2 * BODY)) | (~body & (j == r + 168))
    return ones_where(high), ones_where(low)


def stack_state(q_ref, st_ref):
    for f in range(4):
        cols = slice(f * ELEM, (f + 1) * ELEM)
        high, low = halves(q_ref[f, 0:BODY, :])
        st_ref[0:BODY, cols] = high
        st_ref[BODY : 2 * BODY, cols] = low
        st_ref[2 * BODY : 3 * BODY, cols] = high
        tail = q_ref[f, BODY:NR, :]
        tail_high = tail.astype(BF16).astype(F32)
        tail_low = pltpu.roll(tail - tail_high, 4, 0)
        st_ref[3 * BODY : 256, cols] = jnp.concatenate([tail_high + tail_low, tail_high], axis=0).astype(BF16)


def kernel(
    n_group,
    n_sub,
    fields_hbm,
    diff_hbm,
    interp_hbm,
    lift_hbm,
    jac_hbm,
    scale_hbm,
    angle_hbm,
    reflect_hbm,
    send_hbm,
    recv_hbm,
    class_hbm,
    out_ref,
    fields,
    diff,
    interp,
    lift,
    jac,
    scale,
    angle,
    reflect,
    send,
    recv,
    klass,
    q,
    res,
    st,
    fpad,
    w_face,
    w_diff,
    w_lift,
    sel,
    oh_local,
    oh_far,
    coef,
    jcoef,
    own,
    table,
    upl,
    flux,
    send_buf,
    recv_buf,
    load_sem,
    send_sem,
    recv_sem,
):
    g, s = lax.axis_index("group"), lax.axis_index("sub")
    g_next, g_prev = lax.rem(g + 1, n_group), lax.rem(g + n_group - 1, n_group)
    s_next, s_prev = lax.rem(s + 1, n_sub), lax.rem(s + n_sub - 1, n_sub)
    exists = (s < n_sub - 1, s > 0, g < n_group - 1, g > 0)
    peers = ((g, s_next), (g, s_prev), (g_next, s), (g_prev, s))

    loads = [
        pltpu.make_async_copy(src, dst, load_sem.at[i])
        for i, (src, dst) in enumerate(
            (
                (interp_hbm, interp),
                (fields_hbm, fields),
                (send_hbm, send),
                (recv_hbm, recv),
                (class_hbm, klass),
                (angle_hbm, angle),
                (scale_hbm, scale),
                (reflect_hbm, reflect),
                (jac_hbm, jac),
                (diff_hbm, diff),
                (lift_hbm, lift),
            )
        )
    ]
    for load in loads:
        load.start()
    recv_buf[...] = jnp.zeros_like(recv_buf)
    barrier = pltpu.get_barrier_semaphore()
    for peer, there in zip(peers, exists):

        @pl.when(there)
        def _(peer=peer):
            pl.semaphore_signal(barrier, inc=1, device_id=peer, device_id_type=MESH)


    spread_high, spread_low = spread_nodes()
    fpad[...] = jnp.zeros_like(fpad)
    loads[0].wait()
    rows = jnp.transpose(interp[...], (1, 0))
    for k in range(4):
        fpad[k * FR : k * FR + NFP, :] = rows[k * NFP : (k + 1) * NFP, :]
    high, low = halves(fpad[...])
    w_face[...] = (mm(high, spread_high) + mm(low, spread_low)).astype(BF16)
    loads[1].wait()
    for f in range(4):
        q[f, BODY:NR, :] = jnp.zeros((NR - BODY, ELEM), F32)
        q[f, 0:NP, :] = fields[pl.ds(f, NP, stride=4), :]
    stack_state(q, st)
    loads[2].wait()
    for j in range(4):
        wanted = jnp.transpose(jnp.broadcast_to(send[j : j + 1, :], (CAP, CAP)), (1, 0))[:, 0:1]
        sel[j * CAP : (j + 1) * CAP, :] = ones_where(iota((CAP, FACES), 1) == wanted)

    def copy_to(m, j):
        return pltpu.make_async_remote_copy(
            src_ref=send_buf.at[m, j],
            dst_ref=recv_buf.at[m, j],
            send_sem=send_sem.at[m, j],
            recv_sem=recv_sem.at[m, j],
            device_id=peers[j],
            device_id_type=MESH,
        )

    def face_part(m):
        traces = mm(w_face[...], st[...])
        for f in range(4):
            for k in range(4):
                block = traces[k * FR : (k + 1) * FR, f * ELEM : (f + 1) * ELEM]
                own[f, k] = block
                high, low = halves(block)
                table[f * FR : (f + 1) * FR, k * ELEM : (k + 1) * ELEM] = high
                table[4 * FR + f * FR : 4 * FR + (f + 1) * FR, k * ELEM : (k + 1) * ELEM] = low
        packed = mm_nt(sel[...], table[...])
        packed = packed[:, 0:128] + packed[:, 128:256]
        for j in range(4):
            send_buf[m, j] = packed[j * CAP : (j + 1) * CAP, :]

    def launch(m):
        for j in (2, 3, 0, 1):

            @pl.when(exists[j])
            def _(j=j):
                copy_to(m, j).start()


    def c8(i, k):
        return coef[i, k][None]

    def tile(x):
        return x.reshape(FR // 8, 8, ELEM)

    def local_part(m, a_now):
        vol = None
        for a in range(3):
            slopes = mm(w_diff[a], st[:, ELEM : 4 * ELEM])
            for c in range(3):
                term = slopes[:, c * ELEM : (c + 1) * ELEM].reshape(NR // 8, 8, ELEM) * jcoef[a, c][None]
                vol = term if vol is None else vol + term
        res[0] = a_now * res[0] + vol.reshape(NR, ELEM)
        slopes = [mm(w_diff[a], st[:, 0:ELEM]).reshape(NR // 8, 8, ELEM) for a in range(3)]
        for c in range(3):
            vol = sum(slopes[a] * jcoef[a, c][None] for a in range(3))
            res[1 + c] = a_now * res[1 + c] + vol.reshape(NR, ELEM)
        near = mm(table[...], oh_local[...])
        near = near[0:128, :] + near[128:256, :]
        for k in range(4):
            po, uo, vo, wo = (tile(own[f, k]) for f in range(4))
            pn, un, vn, wn = (
                tile(near[f * FR : (f + 1) * FR, k * ELEM : (k + 1) * ELEM]) for f in range(4)
            )
            nx, ny, nz, sc, rf = (c8(i, k) for i in range(5))
            minus = nx * uo + ny * vo + nz * wo
            got = pn + (nx * un + ny * vn + nz * wn)
            up = sc * (got + rf * (po - minus) - (po + minus))
            upl[k] = up.reshape(FR, ELEM)

    def far_part(m, b_now, last):
        arrived = recv_buf[m].reshape(SLOTS, 128)
        high = arrived.astype(BF16).astype(F32)
        both = jnp.concatenate([high, arrived - high], axis=0)
        far = mm(jnp.transpose(both, (1, 0)).astype(BF16), oh_far[...])
        for k in range(4):
            pn, un, vn, wn = (
                tile(far[f * FR : (f + 1) * FR, k * ELEM : (k + 1) * ELEM]) for f in range(4)
            )
            nx, ny, nz, sc = (c8(i, k) for i in range(4))
            up = tile(upl[k]) + sc * (pn + (nx * un + ny * vn + nz * wn))
            for f, term in enumerate((up, nx * up, ny * up, nz * up)):
                high, low = halves(term.reshape(FR, ELEM))
                flux[k * FR : (k + 1) * FR, f * ELEM : (f + 1) * ELEM] = high
                flux[4 * FR + k * FR : 4 * FR + (k + 1) * FR, f * ELEM : (f + 1) * ELEM] = low
        lifted = mm(w_lift[...], flux[...])
        lifted = lifted[0:NR, :] + lifted[NR : 2 * NR, :]
        for f in range(4):
            change = res[f] + lifted[:, f * ELEM : (f + 1) * ELEM]
            new = q[f] + b_now * change
            res[f] = change
            q[f] = new

    face_part(0)
    pl.semaphore_wait(barrier, sum(e.astype(jnp.int32) for e in exists))
    launch(0)

    for load in loads[3:]:
        load.wait()
    for k in range(4):
        rows = slice(k * ELEM, (k + 1) * ELEM)
        where = jnp.where(klass[k : k + 1, :] == 0, recv[k : k + 1, :], -1)
        oh_local[:, rows] = ones_where(iota((FACES, ELEM), 0) == where)
        slot = iota((2 * SLOTS, ELEM), 0)
        slot = jnp.where(slot >= SLOTS, slot - SLOTS, slot)
        oh_far[:, rows] = ones_where(slot + FACES == where)
        first, second = angle[0, k : k + 1, :], angle[1, k : k + 1, :]
        flat = jnp.cos(second)
        kinds = klass[k : k + 1, :]
        mirror = jnp.zeros((1, ELEM), F32)
        for c in range(4):
            mirror = mirror + jnp.where(kinds == c + 1, reflect[c], 0.0)
        for i, row in enumerate(
            (
                -(jnp.cos(first) * flat),
                -(jnp.sin(first) * flat),
                -jnp.sin(second),
                0.5 * scale[k : k + 1, :],
                mirror,
            )
        ):
            coef[i, k] = jnp.broadcast_to(row, (8, ELEM))
    for a in range(3):
        high, low = halves(diff[a] * (-DT))
        w_diff[a] = jnp.zeros((NR, 256), BF16)
        w_diff[a, 0:NP, :] = (mm(high, spread_high) + mm(low, spread_low)).astype(BF16)
        for c in range(3):
            jcoef[a, c] = jnp.broadcast_to(jac[a, c : c + 1, :], (8, ELEM))
    r, j = iota((4 * NFP, 4 * FR), 0), iota((4 * NFP, 4 * FR), 1)
    face = (r >= NFP).astype(jnp.int32) + (r >= 2 * NFP).astype(jnp.int32) + (r >= 3 * NFP).astype(jnp.int32)
    spread_face = ones_where(j == r + (FR - NFP) * face)
    high, low = halves(lift[...] * DT)
    high, low = mm(high, spread_face).astype(BF16), mm(low, spread_face).astype(BF16)
    w_lift[...] = jnp.zeros_like(w_lift)
    w_lift[0:NP, 0:128] = high
    w_lift[0:NP, 128:256] = high
    w_lift[NR : NR + NP, 0:128] = low
    for f in range(4):
        res[f] = jnp.zeros((NR, ELEM), F32)

    def finish(m, b_now):
        for j in (0, 1, 2, 3):

            @pl.when(exists[j ^ 1])
            def _(j=j):
                copy_to(m, j).wait_recv()

        far_part(m, b_now, False)

    def pick(values, m):
        out = jnp.float32(values[0])
        for i in range(1, SECTIONS):
            out = jnp.where(m == i, jnp.float32(values[i]), out)
        return out

    def section(m, carry):
        local_part(m - 1, pick(RK_A, m - 1))
        finish(m - 1, pick(RK_B, m - 1))
        stack_state(q, st)
        face_part(m)
        launch(m)
        return carry

    lax.fori_loop(1, SECTIONS, section, 0)
    local_part(SECTIONS - 1, RK_A[-1])
    finish(SECTIONS - 1, RK_B[-1])
    for j in range(4):

        @pl.when(exists[j])
        def _(j=j):
            for m in range(SECTIONS):
                copy_to(m, j).wait_send()

    for f in range(4):
        out_ref[pl.ds(f, NP, stride=4), :] = q[f, 0:NP, :]


def shards(n_group, n_sub, fields, diff_ops, face_interp, *rest):
    rows = jnp.transpose(fields, (1, 0, 2)).reshape(4 * NP, ELEM)
    args = (rows, diff_ops, jnp.transpose(face_interp, (1, 0))) + rest
    vm = pltpu.VMEM
    loaded = [
        pltpu.SMEM(x.shape, x.dtype) if i == 7 else vm(x.shape, x.dtype) for i, x in enumerate(args)
    ]
    out = pl.pallas_call(
        functools.partial(kernel, n_group, n_sub),
        out_shape=jax.ShapeDtypeStruct(rows.shape, F32),
        in_specs=[pl.BlockSpec(memory_space=pl.ANY)] * len(args),
        out_specs=pl.BlockSpec(memory_space=pltpu.VMEM),
        scratch_shapes=loaded
        + [
            vm((4, NR, ELEM), F32),
            vm((4, NR, ELEM), F32),
            vm((256, FACES), BF16),
            vm((4 * FR, NP), F32),
            vm((4 * FR, 256), BF16),
            vm((3, NR, 256), BF16),
            vm((2 * NR, 256), BF16),
            vm((SLOTS, FACES), BF16),
            vm((FACES, FACES), BF16),
            vm((2 * SLOTS, FACES), BF16),
            vm((5, 4, 8, ELEM), F32),
            vm((3, 3, 8, ELEM), F32),
            vm((4, 4, FR, ELEM), F32),
            vm((256, FACES), BF16),
            vm((4, FR, ELEM), F32),
            vm((256, FACES), BF16),
            vm((SECTIONS, 4, CAP, 128), F32),
            vm((SECTIONS, 4, CAP, 128), F32),
            pltpu.SemaphoreType.DMA((len(args),)),
            pltpu.SemaphoreType.DMA((SECTIONS, 4)),
            pltpu.SemaphoreType.DMA((SECTIONS, 4)),
        ],
        compiler_params=pltpu.CompilerParams(collective_id=0, has_side_effects=True),
        name="sections",
    )(*args)
    return jnp.transpose(out.reshape(NP, 4, ELEM), (1, 0, 2))


def solution(mesh):
    both = ("group", "sub")
    return jax.shard_map(
        functools.partial(shards, mesh.shape["group"], mesh.shape["sub"]),
        mesh=mesh,
        in_specs=(
            P(None, None, both),
            P(),
            P(),
            P(),
            P(None, None, both),
            P(None, both),
            P(None, None, both),
            P(),
            P(None, both),
            P(None, both),
            P(None, both),
        ),
        out_specs=P(None, None, both),
        check_vma=False,
    )
```

```python
import functools

import jax
import jax.numpy as jnp
from jax import lax
from jax.experimental import pallas as pl
from jax.experimental.pallas import tpu as pltpu
from jax.sharding import PartitionSpec as P

MESH = pl.DeviceIdType.MESH
F32 = jnp.float32
BF16 = jnp.bfloat16
RK_A = (
    0.0,
    -567301805773.0 / 1357537059087.0,
    -2404267990393.0 / 2016746695238.0,
    -3550918686646.0 / 2091501179385.0,
    -1275806237668.0 / 842570457699.0,
)
RK_B = (
    1432997174477.0 / 9575080441755.0,
    5161836677717.0 / 13612068292357.0,
    1720146321549.0 / 2090206949498.0,
    3134564353537.0 / 4481467310338.0,
    2277821191437.0 / 14882151754819.0,
)
DT = 0.3
SECTIONS = 5
NP = 84
NR = 88
FR = 32
NFP = 28
ELEM = 128
FACES = 4 * ELEM
CAP = 16
SLOTS = 4 * CAP
BODY = 80


def iota(shape, dim):
    return lax.broadcasted_iota(jnp.int32, shape, dim)


def ones_where(cond):
    return jnp.where(cond, 1.0, 0.0).astype(BF16)


def halves(x):
    high = x.astype(BF16)
    return high, (x - high.astype(F32)).astype(BF16)


def mm(a, b):
    return jnp.dot(a, b, preferred_element_type=F32)


def mm_nt(a, b):
    return lax.dot_general(a, b, (((1,), (1,)), ((), ())), preferred_element_type=F32)


def spread_nodes():
    r, j = iota((NP, 256), 0), iota((NP, 256), 1)
    body = r < BODY
    high = (body & ((j == r) | (j == r + BODY))) | (~body & ((j == r + 160) | (j == r + 164)))
    low = (body & (j == r + 2 * BODY)) | (~body & (j == r + 168))
    return ones_where(high), ones_where(low)


def stack_state(q_ref, st_ref):
    for f in range(4):
        cols = slice(f * ELEM, (f + 1) * ELEM)
        high, low = halves(q_ref[f, 0:BODY, :])
        st_ref[0:BODY, cols] = high
        st_ref[BODY : 2 * BODY, cols] = low
        st_ref[2 * BODY : 3 * BODY, cols] = high
        tail = q_ref[f, BODY:NR, :]
        tail_high = tail.astype(BF16).astype(F32)
        tail_low = pltpu.roll(tail - tail_high, 4, 0)
        st_ref[3 * BODY : 256, cols] = jnp.concatenate([tail_high + tail_low, tail_high], axis=0).astype(BF16)


def kernel(
    n_group,
    n_sub,
    fields_hbm,
    diff_hbm,
    interp_hbm,
    lift_hbm,
    jac_hbm,
    scale_hbm,
    angle_hbm,
    reflect_hbm,
    send_hbm,
    recv_hbm,
    class_hbm,
    out_ref,
    fields,
    diff,
    interp,
    lift,
    jac,
    scale,
    angle,
    reflect,
    send,
    recv,
    klass,
    q,
    res,
    st,
    fpad,
    w_face,
    w_diff,
    w_lift,
    sel,
    oh_local,
    oh_far,
    coef,
    jcoef,
    own,
    table,
    upl,
    flux,
    send_buf,
    recv_buf,
    load_sem,
    send_sem,
    recv_sem,
):
    g, s = lax.axis_index("group"), lax.axis_index("sub")
    g_next, g_prev = lax.rem(g + 1, n_group), lax.rem(g + n_group - 1, n_group)
    s_next, s_prev = lax.rem(s + 1, n_sub), lax.rem(s + n_sub - 1, n_sub)
    exists = (s < n_sub - 1, s > 0, g < n_group - 1, g > 0)
    peers = ((g, s_next), (g, s_prev), (g_next, s), (g_prev, s))

    loads = [
        pltpu.make_async_copy(src, dst, load_sem.at[i])
        for i, (src, dst) in enumerate(
            (
                (interp_hbm, interp),
                (fields_hbm, fields),
                (send_hbm, send),
                (recv_hbm, recv),
                (class_hbm, klass),
                (angle_hbm, angle),
                (scale_hbm, scale),
                (reflect_hbm, reflect),
                (jac_hbm, jac),
                (diff_hbm, diff),
                (lift_hbm, lift),
            )
        )
    ]
    for load in loads:
        load.start()
    recv_buf[...] = jnp.zeros_like(recv_buf)
    barrier = pltpu.get_barrier_semaphore()
    for peer, there in zip(peers, exists):

        @pl.when(there)
        def _(peer=peer):
            pl.semaphore_signal(barrier, inc=1, device_id=peer, device_id_type=MESH)


    spread_high, spread_low = spread_nodes()
    fpad[...] = jnp.zeros_like(fpad)
    loads[0].wait()
    rows = jnp.transpose(interp[...], (1, 0))
    for k in range(4):
        fpad[k * FR : k * FR + NFP, :] = rows[k * NFP : (k + 1) * NFP, :]
    high, low = halves(fpad[...])
    w_face[...] = (mm(high, spread_high) + mm(low, spread_low)).astype(BF16)
    loads[1].wait()
    for f in range(4):
        q[f, BODY:NR, :] = jnp.zeros((NR - BODY, ELEM), F32)
        q[f, 0:NP, :] = fields[pl.ds(f, NP, stride=4), :]
    stack_state(q, st)
    loads[2].wait()
    for j in range(4):
        wanted = jnp.transpose(jnp.broadcast_to(send[j : j + 1, :], (CAP, CAP)), (1, 0))[:, 0:1]
        sel[j * CAP : (j + 1) * CAP, :] = ones_where(iota((CAP, FACES), 1) == wanted)

    def copy_to(m, j):
        return pltpu.make_async_remote_copy(
            src_ref=send_buf.at[m, j],
            dst_ref=recv_buf.at[m, j],
            send_sem=send_sem.at[m, j],
            recv_sem=recv_sem.at[m, j],
            device_id=peers[j],
            device_id_type=MESH,
        )

    def face_part(m):
        traces = mm(w_face[...], st[...])
        for f in range(4):
            for k in range(4):
                block = traces[k * FR : (k + 1) * FR, f * ELEM : (f + 1) * ELEM]
                own[f, k] = block
                high, low = halves(block)
                table[f * FR : (f + 1) * FR, k * ELEM : (k + 1) * ELEM] = high
                table[4 * FR + f * FR : 4 * FR + (f + 1) * FR, k * ELEM : (k + 1) * ELEM] = low
        packed = mm_nt(sel[...], table[...])
        packed = packed[:, 0:128] + packed[:, 128:256]
        for j in range(4):
            send_buf[m, j] = packed[j * CAP : (j + 1) * CAP, :]

    def launch(m):
        for j in (2, 3, 0, 1):

            @pl.when(exists[j])
            def _(j=j):
                copy_to(m, j).start()


    def c8(i, k):
        return coef[i, k][None]

    def tile(x):
        return x.reshape(FR // 8, 8, ELEM)

    def local_part(m, a_now):
        vol = None
        for a in range(3):
            slopes = mm(w_diff[a], st[:, ELEM : 4 * ELEM])
            for c in range(3):
                term = slopes[:, c * ELEM : (c + 1) * ELEM].reshape(NR // 8, 8, ELEM) * jcoef[a, c][None]
                vol = term if vol is None else vol + term
        res[0] = a_now * res[0] + vol.reshape(NR, ELEM)
        slopes = [mm(w_diff[a], st[:, 0:ELEM]).reshape(NR // 8, 8, ELEM) for a in range(3)]
        for c in range(3):
            vol = sum(slopes[a] * jcoef[a, c][None] for a in range(3))
            res[1 + c] = a_now * res[1 + c] + vol.reshape(NR, ELEM)
        near = mm(table[...], oh_local[...])
        near = near[0:128, :] + near[128:256, :]
        for k in range(4):
            po, uo, vo, wo = (tile(own[f, k]) for f in range(4))
            pn, un, vn, wn = (
                tile(near[f * FR : (f + 1) * FR, k * ELEM : (k + 1) * ELEM]) for f in range(4)
            )
            nx, ny, nz, sc, rf = (c8(i, k) for i in range(5))
            minus = nx * uo + ny * vo + nz * wo
            got = pn + (nx * un + ny * vn + nz * wn)
            up = sc * (got + rf * (po - minus) - (po + minus))
            upl[k] = up.reshape(FR, ELEM)

    def far_part(m, b_now, last):
        arrived = recv_buf[m].reshape(SLOTS, 128)
        high = arrived.astype(BF16).astype(F32)
        both = jnp.concatenate([high, arrived - high], axis=0)
        far = mm(jnp.transpose(both, (1, 0)).astype(BF16), oh_far[...])
        for k in range(4):
            pn, un, vn, wn = (
                tile(far[f * FR : (f + 1) * FR, k * ELEM : (k + 1) * ELEM]) for f in range(4)
            )
            nx, ny, nz, sc = (c8(i, k) for i in range(4))
            up = tile(upl[k]) + sc * (pn + (nx * un + ny * vn + nz * wn))
            for f, term in enumerate((up, nx * up, ny * up, nz * up)):
                high, low = halves(term.reshape(FR, ELEM))
                flux[k * FR : (k + 1) * FR, f * ELEM : (f + 1) * ELEM] = high
                flux[4 * FR + k * FR : 4 * FR + (k + 1) * FR, f * ELEM : (f + 1) * ELEM] = low
        lifted = mm(w_lift[...], flux[...])
        lifted = lifted[0:NR, :] + lifted[NR : 2 * NR, :]
        for f in range(4):
            change = res[f] + lifted[:, f * ELEM : (f + 1) * ELEM]
            new = q[f] + b_now * change
            res[f] = change
            q[f] = new

    face_part(0)
    pl.semaphore_wait(barrier, sum(e.astype(jnp.int32) for e in exists))
    launch(0)

    for load in loads[3:]:
        load.wait()
    for k in range(4):
        rows = slice(k * ELEM, (k + 1) * ELEM)
        where = jnp.where(klass[k : k + 1, :] == 0, recv[k : k + 1, :], -1)
        oh_local[:, rows] = ones_where(iota((FACES, ELEM), 0) == where)
        slot = iota((2 * SLOTS, ELEM), 0)
        slot = jnp.where(slot >= SLOTS, slot - SLOTS, slot)
        oh_far[:, rows] = ones_where(slot + FACES == where)
        first, second = angle[0, k : k + 1, :], angle[1, k : k + 1, :]
        flat = jnp.cos(second)
        kinds = klass[k : k + 1, :]
        mirror = jnp.zeros((1, ELEM), F32)
        for c in range(4):
            mirror = mirror + jnp.where(kinds == c + 1, reflect[c], 0.0)
        for i, row in enumerate(
            (
                -(jnp.cos(first) * flat),
                -(jnp.sin(first) * flat),
                -jnp.sin(second),
                0.5 * scale[k : k + 1, :],
                mirror,
            )
        ):
            coef[i, k] = jnp.broadcast_to(row, (8, ELEM))
    for a in range(3):
        high, low = halves(diff[a] * (-DT))
        w_diff[a] = jnp.zeros((NR, 256), BF16)
        w_diff[a, 0:NP, :] = (mm(high, spread_high) + mm(low, spread_low)).astype(BF16)
        for c in range(3):
            jcoef[a, c] = jnp.broadcast_to(jac[a, c : c + 1, :], (8, ELEM))
    r, j = iota((4 * NFP, 4 * FR), 0), iota((4 * NFP, 4 * FR), 1)
    face = (r >= NFP).astype(jnp.int32) + (r >= 2 * NFP).astype(jnp.int32) + (r >= 3 * NFP).astype(jnp.int32)
    spread_face = ones_where(j == r + (FR - NFP) * face)
    high, low = halves(lift[...] * DT)
    high, low = mm(high, spread_face).astype(BF16), mm(low, spread_face).astype(BF16)
    w_lift[...] = jnp.zeros_like(w_lift)
    w_lift[0:NP, 0:128] = high
    w_lift[0:NP, 128:256] = high
    w_lift[NR : NR + NP, 0:128] = low
    for f in range(4):
        res[f] = jnp.zeros((NR, ELEM), F32)

    def finish(m, b_now):
        for j in (0, 1, 2, 3):

            @pl.when(exists[j ^ 1])
            def _(j=j):
                copy_to(m, j).wait_recv()

        far_part(m, b_now, False)

    def pick(values, m):
        out = jnp.float32(values[0])
        for i in range(1, SECTIONS):
            out = jnp.where(m == i, jnp.float32(values[i]), out)
        return out

    def section(m, carry):
        local_part(m - 1, pick(RK_A, m - 1))
        finish(m - 1, pick(RK_B, m - 1))
        stack_state(q, st)
        face_part(m)
        launch(m)
        return carry

    lax.fori_loop(1, SECTIONS, section, 0)
    local_part(SECTIONS - 1, RK_A[-1])
    finish(SECTIONS - 1, RK_B[-1])
    for j in range(4):

        @pl.when(exists[j])
        def _(j=j):
            for m in range(SECTIONS):
                copy_to(m, j).wait_send()

    for f in range(4):
        out_ref[pl.ds(f, NP, stride=4), :] = q[f, 0:NP, :]


def hand_on(x_ref, out_ref, sem):
    copy = pltpu.make_async_copy(x_ref, out_ref, sem)
    copy.start()
    copy.wait()


def shards(n_group, n_sub, fields, diff_ops, face_interp, *rest):
    rows = jnp.transpose(fields, (1, 0, 2)).reshape(4 * NP, ELEM)
    args = (rows, diff_ops, jnp.transpose(face_interp, (1, 0))) + rest
    vm = pltpu.VMEM
    loaded = [
        pltpu.SMEM(x.shape, x.dtype) if i == 7 else vm(x.shape, x.dtype) for i, x in enumerate(args)
    ]
    args = tuple(pltpu.with_memory_space_constraint(x, pltpu.HBM) for x in args)
    out = pl.pallas_call(
        functools.partial(kernel, n_group, n_sub),
        out_shape=jax.ShapeDtypeStruct(rows.shape, F32),
        in_specs=[pl.BlockSpec(memory_space=pl.ANY)] * len(args),
        out_specs=pl.BlockSpec(memory_space=pltpu.VMEM),
        scratch_shapes=loaded
        + [
            vm((4, NR, ELEM), F32),
            vm((4, NR, ELEM), F32),
            vm((256, FACES), BF16),
            vm((4 * FR, NP), F32),
            vm((4 * FR, 256), BF16),
            vm((3, NR, 256), BF16),
            vm((2 * NR, 256), BF16),
            vm((SLOTS, FACES), BF16),
            vm((FACES, FACES), BF16),
            vm((2 * SLOTS, FACES), BF16),
            vm((5, 4, 8, ELEM), F32),
            vm((3, 3, 8, ELEM), F32),
            vm((4, 4, FR, ELEM), F32),
            vm((256, FACES), BF16),
            vm((4, FR, ELEM), F32),
            vm((256, FACES), BF16),
            vm((SECTIONS, 4, CAP, 128), F32),
            vm((SECTIONS, 4, CAP, 128), F32),
            pltpu.SemaphoreType.DMA((len(args),)),
            pltpu.SemaphoreType.DMA((SECTIONS, 4)),
            pltpu.SemaphoreType.DMA((SECTIONS, 4)),
        ],
        compiler_params=pltpu.CompilerParams(
            collective_id=0, has_side_effects=True, vmem_limit_bytes=16 << 20
        ),
        name="sections",
    )(*args)
    out = pl.pallas_call(
        hand_on,
        out_shape=jax.ShapeDtypeStruct(out.shape, F32),
        in_specs=[pl.BlockSpec(memory_space=pltpu.VMEM)],
        out_specs=pl.BlockSpec(memory_space=pl.ANY),
        scratch_shapes=[pltpu.SemaphoreType.DMA],
        compiler_params=pltpu.CompilerParams(vmem_limit_bytes=8 << 20),
        name="hand_on",
    )(out)
    return jnp.transpose(out.reshape(NP, 4, ELEM), (1, 0, 2))


def solution(mesh):
    both = ("group", "sub")
    return jax.shard_map(
        functools.partial(shards, mesh.shape["group"], mesh.shape["sub"]),
        mesh=mesh,
        in_specs=(
            P(None, None, both),
            P(),
            P(),
            P(),
            P(None, None, both),
            P(None, both),
            P(None, None, both),
            P(),
            P(None, both),
            P(None, both),
            P(None, both),
        ),
        out_specs=P(None, None, both),
        check_vma=False,
    )
```

```python
import functools

import jax
import jax.numpy as jnp
from jax import lax
from jax.experimental import pallas as pl
from jax.experimental.pallas import tpu as pltpu
from jax.sharding import PartitionSpec as P

MESH = pl.DeviceIdType.MESH
F32 = jnp.float32
BF16 = jnp.bfloat16
RK_A = (
    0.0,
    -567301805773.0 / 1357537059087.0,
    -2404267990393.0 / 2016746695238.0,
    -3550918686646.0 / 2091501179385.0,
    -1275806237668.0 / 842570457699.0,
)
RK_B = (
    1432997174477.0 / 9575080441755.0,
    5161836677717.0 / 13612068292357.0,
    1720146321549.0 / 2090206949498.0,
    3134564353537.0 / 4481467310338.0,
    2277821191437.0 / 14882151754819.0,
)
DT = 0.3
SECTIONS = 5
NP = 84
NR = 88
FR = 32
NFP = 28
ELEM = 128
FACES = 4 * ELEM
CAP = 16
SLOTS = 4 * CAP
BODY = 80


def iota(shape, dim):
    return lax.broadcasted_iota(jnp.int32, shape, dim)


def ones_where(cond):
    return jnp.where(cond, 1.0, 0.0).astype(BF16)


def halves(x):
    high = x.astype(BF16)
    return high, (x - high.astype(F32)).astype(BF16)


def mm(a, b):
    return jnp.dot(a, b, preferred_element_type=F32)


def mm_nt(a, b):
    return lax.dot_general(a, b, (((1,), (1,)), ((), ())), preferred_element_type=F32)


def spread_nodes():
    r, j = iota((NP, 256), 0), iota((NP, 256), 1)
    body = r < BODY
    high = (body & ((j == r) | (j == r + BODY))) | (~body & ((j == r + 160) | (j == r + 164)))
    low = (body & (j == r + 2 * BODY)) | (~body & (j == r + 168))
    return ones_where(high), ones_where(low)


def stack_state(q_ref):
    columns = []
    for f in range(4):
        high, low = halves(q_ref[f, 0:BODY, :])
        tail = q_ref[f, BODY:NR, :]
        tail_high = tail.astype(BF16).astype(F32)
        tail_low = pltpu.roll(tail - tail_high, 4, 0)
        tails = jnp.concatenate([tail_high + tail_low, tail_high], axis=0).astype(BF16)
        columns.append(jnp.concatenate([high, low, high, tails], axis=0))
    return jnp.concatenate(columns, axis=1)


def kernel(
    n_group,
    n_sub,
    fields_hbm,
    diff_hbm,
    interp_hbm,
    lift_hbm,
    jac_hbm,
    scale_hbm,
    angle_hbm,
    reflect_hbm,
    send_hbm,
    recv_hbm,
    class_hbm,
    out_ref,
    fields,
    diff,
    interp,
    lift,
    jac,
    scale,
    angle,
    reflect,
    send,
    recv,
    klass,
    q,
    res,
    st,
    fpad,
    w_face,
    w_diff,
    w_lift,
    sel,
    oh_local,
    oh_far,
    coef,
    jcoef,
    own,
    table,
    upl,
    send_buf,
    recv_buf,
    load_sem,
    send_sem,
    recv_sem,
):
    g, s = lax.axis_index("group"), lax.axis_index("sub")
    g_next, g_prev = lax.rem(g + 1, n_group), lax.rem(g + n_group - 1, n_group)
    s_next, s_prev = lax.rem(s + 1, n_sub), lax.rem(s + n_sub - 1, n_sub)
    exists = (s < n_sub - 1, s > 0, g < n_group - 1, g > 0)
    peers = ((g, s_next), (g, s_prev), (g_next, s), (g_prev, s))

    loads = [
        pltpu.make_async_copy(src, dst, load_sem.at[i])
        for i, (src, dst) in enumerate(
            (
                (interp_hbm, interp),
                (fields_hbm, fields),
                (send_hbm, send),
                (recv_hbm, recv),
                (class_hbm, klass),
                (angle_hbm, angle),
                (scale_hbm, scale),
                (reflect_hbm, reflect),
                (jac_hbm, jac),
                (diff_hbm, diff),
                (lift_hbm, lift),
            )
        )
    ]
    for load in loads:
        load.start()
    recv_buf[...] = jnp.zeros_like(recv_buf)
    barrier = pltpu.get_barrier_semaphore()
    for peer, there in zip(peers, exists):

        @pl.when(there)
        def _(peer=peer):
            pl.semaphore_signal(barrier, inc=1, device_id=peer, device_id_type=MESH)


    spread_high, spread_low = spread_nodes()
    fpad[...] = jnp.zeros_like(fpad)
    loads[0].wait()
    rows = jnp.transpose(interp[...], (1, 0))
    for k in range(4):
        fpad[k * FR : k * FR + NFP, :] = rows[k * NFP : (k + 1) * NFP, :]
    high, low = halves(fpad[...])
    w_face[...] = (mm(high, spread_high) + mm(low, spread_low)).astype(BF16)
    loads[1].wait()
    for f in range(4):
        q[f, BODY:NR, :] = jnp.zeros((NR - BODY, ELEM), F32)
        q[f, 0:NP, :] = fields[pl.ds(f, NP, stride=4), :]
    loads[2].wait()
    for j in range(4):
        wanted = jnp.transpose(jnp.broadcast_to(send[j : j + 1, :], (CAP, CAP)), (1, 0))[:, 0:1]
        sel[j * CAP : (j + 1) * CAP, :] = ones_where(iota((CAP, FACES), 1) == wanted)

    def copy_to(m, j):
        return pltpu.make_async_remote_copy(
            src_ref=send_buf.at[m, j],
            dst_ref=recv_buf.at[m, j],
            send_sem=send_sem.at[m, j],
            recv_sem=recv_sem.at[m, j],
            device_id=peers[j],
            device_id_type=MESH,
        )

    def face_part(m):
        state = stack_state(q)
        traces = mm(w_face[...], state)
        st[...] = state
        blocks = {}
        for f in range(4):
            for k in range(4):
                block = traces[k * FR : (k + 1) * FR, f * ELEM : (f + 1) * ELEM]
                own[f, k] = block
                blocks[0, f, k], blocks[1, f, k] = halves(block)
        whole = jnp.concatenate(
            [
                jnp.concatenate([blocks[h, f, k] for k in range(4)], axis=1)
                for h in range(2)
                for f in range(4)
            ],
            axis=0,
        )
        packed = mm_nt(sel[...], whole)
        table[...] = whole
        packed = packed[:, 0:128] + packed[:, 128:256]
        for j in range(4):
            send_buf[m, j] = packed[j * CAP : (j + 1) * CAP, :]

    def launch(m):
        for j in (2, 3, 0, 1):

            @pl.when(exists[j])
            def _(j=j):
                copy_to(m, j).start()


    def c8(i, k):
        return coef[i, k][None]

    def tile(x):
        return x.reshape(FR // 8, 8, ELEM)

    def local_part(m, a_now):
        vol = None
        for a in range(3):
            slopes = mm(w_diff[a], st[:, ELEM : 4 * ELEM])
            for c in range(3):
                term = slopes[:, c * ELEM : (c + 1) * ELEM].reshape(NR // 8, 8, ELEM) * jcoef[a, c][None]
                vol = term if vol is None else vol + term
        res[0] = a_now * res[0] + vol.reshape(NR, ELEM)
        slopes = [mm(w_diff[a], st[:, 0:ELEM]).reshape(NR // 8, 8, ELEM) for a in range(3)]
        for c in range(3):
            vol = sum(slopes[a] * jcoef[a, c][None] for a in range(3))
            res[1 + c] = a_now * res[1 + c] + vol.reshape(NR, ELEM)
        near = mm(table[...], oh_local[...])
        near = near[0:128, :] + near[128:256, :]
        for k in range(4):
            po, uo, vo, wo = (tile(own[f, k]) for f in range(4))
            pn, un, vn, wn = (
                tile(near[f * FR : (f + 1) * FR, k * ELEM : (k + 1) * ELEM]) for f in range(4)
            )
            nx, ny, nz, sc, rf = (c8(i, k) for i in range(5))
            minus = nx * uo + ny * vo + nz * wo
            got = pn + (nx * un + ny * vn + nz * wn)
            up = sc * (got + rf * (po - minus) - (po + minus))
            upl[k] = up.reshape(FR, ELEM)

    def far_part(m, b_now, last):
        arrived = recv_buf[m].reshape(SLOTS, 128)
        high = arrived.astype(BF16).astype(F32)
        both = jnp.concatenate([high, arrived - high], axis=0)
        far = mm(jnp.transpose(both, (1, 0)).astype(BF16), oh_far[...])
        parts = {}
        for k in range(4):
            pn, un, vn, wn = (
                tile(far[f * FR : (f + 1) * FR, k * ELEM : (k + 1) * ELEM]) for f in range(4)
            )
            nx, ny, nz, sc = (c8(i, k) for i in range(4))
            up = tile(upl[k]) + sc * (pn + (nx * un + ny * vn + nz * wn))
            for f, term in enumerate((up, nx * up, ny * up, nz * up)):
                parts[0, k, f], parts[1, k, f] = halves(term.reshape(FR, ELEM))
        flux = jnp.concatenate(
            [
                jnp.concatenate([parts[h, k, f] for f in range(4)], axis=1)
                for h in range(2)
                for k in range(4)
            ],
            axis=0,
        )
        lifted = mm(w_lift[...], flux)
        lifted = lifted[0:NR, :] + lifted[NR : 2 * NR, :]
        for f in range(4):
            change = res[f] + lifted[:, f * ELEM : (f + 1) * ELEM]
            new = q[f] + b_now * change
            res[f] = change
            q[f] = new

    face_part(0)
    pl.semaphore_wait(barrier, sum(e.astype(jnp.int32) for e in exists))
    launch(0)

    for load in loads[3:]:
        load.wait()
    for k in range(4):
        rows = slice(k * ELEM, (k + 1) * ELEM)
        where = jnp.where(klass[k : k + 1, :] == 0, recv[k : k + 1, :], -1)
        oh_local[:, rows] = ones_where(iota((FACES, ELEM), 0) == where)
        slot = iota((2 * SLOTS, ELEM), 0)
        slot = jnp.where(slot >= SLOTS, slot - SLOTS, slot)
        oh_far[:, rows] = ones_where(slot + FACES == where)
        first, second = angle[0, k : k + 1, :], angle[1, k : k + 1, :]
        flat = jnp.cos(second)
        kinds = klass[k : k + 1, :]
        mirror = jnp.zeros((1, ELEM), F32)
        for c in range(4):
            mirror = mirror + jnp.where(kinds == c + 1, reflect[c], 0.0)
        for i, row in enumerate(
            (
                -(jnp.cos(first) * flat),
                -(jnp.sin(first) * flat),
                -jnp.sin(second),
                0.5 * scale[k : k + 1, :],
                mirror,
            )
        ):
            coef[i, k] = jnp.broadcast_to(row, (8, ELEM))
    for a in range(3):
        high, low = halves(diff[a] * (-DT))
        w_diff[a] = jnp.zeros((NR, 256), BF16)
        w_diff[a, 0:NP, :] = (mm(high, spread_high) + mm(low, spread_low)).astype(BF16)
        for c in range(3):
            jcoef[a, c] = jnp.broadcast_to(jac[a, c : c + 1, :], (8, ELEM))
    r, j = iota((4 * NFP, 4 * FR), 0), iota((4 * NFP, 4 * FR), 1)
    face = (r >= NFP).astype(jnp.int32) + (r >= 2 * NFP).astype(jnp.int32) + (r >= 3 * NFP).astype(jnp.int32)
    spread_face = ones_where(j == r + (FR - NFP) * face)
    high, low = halves(lift[...] * DT)
    high, low = mm(high, spread_face).astype(BF16), mm(low, spread_face).astype(BF16)
    w_lift[...] = jnp.zeros_like(w_lift)
    w_lift[0:NP, 0:128] = high
    w_lift[0:NP, 128:256] = high
    w_lift[NR : NR + NP, 0:128] = low
    for f in range(4):
        res[f] = jnp.zeros((NR, ELEM), F32)

    def finish(m, b_now):
        for j in (0, 1, 2, 3):

            @pl.when(exists[j ^ 1])
            def _(j=j):
                copy_to(m, j).wait_recv()

        far_part(m, b_now, False)

    def pick(values, m):
        out = jnp.float32(values[0])
        for i in range(1, SECTIONS):
            out = jnp.where(m == i, jnp.float32(values[i]), out)
        return out

    def section(m, carry):
        local_part(m - 1, pick(RK_A, m - 1))
        finish(m - 1, pick(RK_B, m - 1))
        face_part(m)
        launch(m)
        return carry

    lax.fori_loop(1, SECTIONS, section, 0)
    local_part(SECTIONS - 1, RK_A[-1])
    finish(SECTIONS - 1, RK_B[-1])
    for j in range(4):

        @pl.when(exists[j])
        def _(j=j):
            for m in range(SECTIONS):
                copy_to(m, j).wait_send()

    for f in range(4):
        out_ref[pl.ds(f, NP, stride=4), :] = q[f, 0:NP, :]


def hand_on(x_ref, out_ref, sem):
    copy = pltpu.make_async_copy(x_ref, out_ref, sem)
    copy.start()
    copy.wait()


def shards(n_group, n_sub, fields, diff_ops, face_interp, *rest):
    rows = jnp.transpose(fields, (1, 0, 2)).reshape(4 * NP, ELEM)
    args = (rows, diff_ops, jnp.transpose(face_interp, (1, 0))) + rest
    vm = pltpu.VMEM
    loaded = [
        pltpu.SMEM(x.shape, x.dtype) if i == 7 else vm(x.shape, x.dtype) for i, x in enumerate(args)
    ]
    args = tuple(pltpu.with_memory_space_constraint(x, pltpu.HBM) for x in args)
    out = pl.pallas_call(
        functools.partial(kernel, n_group, n_sub),
        out_shape=jax.ShapeDtypeStruct(rows.shape, F32),
        in_specs=[pl.BlockSpec(memory_space=pl.ANY)] * len(args),
        out_specs=pl.BlockSpec(memory_space=pltpu.VMEM),
        scratch_shapes=loaded
        + [
            vm((4, NR, ELEM), F32),
            vm((4, NR, ELEM), F32),
            vm((256, FACES), BF16),
            vm((4 * FR, NP), F32),
            vm((4 * FR, 256), BF16),
            vm((3, NR, 256), BF16),
            vm((2 * NR, 256), BF16),
            vm((SLOTS, FACES), BF16),
            vm((FACES, FACES), BF16),
            vm((2 * SLOTS, FACES), BF16),
            vm((5, 4, 8, ELEM), F32),
            vm((3, 3, 8, ELEM), F32),
            vm((4, 4, FR, ELEM), F32),
            vm((256, FACES), BF16),
            vm((4, FR, ELEM), F32),
            vm((SECTIONS, 4, CAP, 128), F32),
            vm((SECTIONS, 4, CAP, 128), F32),
            pltpu.SemaphoreType.DMA((len(args),)),
            pltpu.SemaphoreType.DMA((SECTIONS, 4)),
            pltpu.SemaphoreType.DMA((SECTIONS, 4)),
        ],
        compiler_params=pltpu.CompilerParams(
            collective_id=0, has_side_effects=True, vmem_limit_bytes=16 << 20
        ),
        name="sections",
    )(*args)
    out = pl.pallas_call(
        hand_on,
        out_shape=jax.ShapeDtypeStruct(out.shape, F32),
        in_specs=[pl.BlockSpec(memory_space=pltpu.VMEM)],
        out_specs=pl.BlockSpec(memory_space=pl.ANY),
        scratch_shapes=[pltpu.SemaphoreType.DMA],
        compiler_params=pltpu.CompilerParams(vmem_limit_bytes=8 << 20),
        name="hand_on",
    )(out)
    return jnp.transpose(out.reshape(NP, 4, ELEM), (1, 0, 2))


def solution(mesh):
    both = ("group", "sub")
    return jax.shard_map(
        functools.partial(shards, mesh.shape["group"], mesh.shape["sub"]),
        mesh=mesh,
        in_specs=(
            P(None, None, both),
            P(),
            P(),
            P(),
            P(None, None, both),
            P(None, both),
            P(None, None, both),
            P(),
            P(None, both),
            P(None, both),
            P(None, both),
        ),
        out_specs=P(None, None, both),
        check_vma=False,
    )
```

```python
import functools

import jax
import jax.numpy as jnp
from jax import lax
from jax.experimental import pallas as pl
from jax.experimental.pallas import tpu as pltpu
from jax.sharding import PartitionSpec as P

MESH = pl.DeviceIdType.MESH
F32 = jnp.float32
BF16 = jnp.bfloat16
RK_A = (
    0.0,
    -567301805773.0 / 1357537059087.0,
    -2404267990393.0 / 2016746695238.0,
    -3550918686646.0 / 2091501179385.0,
    -1275806237668.0 / 842570457699.0,
)
RK_B = (
    1432997174477.0 / 9575080441755.0,
    5161836677717.0 / 13612068292357.0,
    1720146321549.0 / 2090206949498.0,
    3134564353537.0 / 4481467310338.0,
    2277821191437.0 / 14882151754819.0,
)
DT = 0.3
SECTIONS = 5
NP = 84
NR = 88
FR = 32
NFP = 28
ELEM = 128
FACES = 4 * ELEM
CAP = 16
SLOTS = 4 * CAP
POS = (0, 2, 1, 3)
BODY = 80


def iota(shape, dim):
    return lax.broadcasted_iota(jnp.int32, shape, dim)


def ones_where(cond):
    return jnp.where(cond, 1.0, 0.0).astype(BF16)


def halves(x):
    high = x.astype(BF16)
    return high, (x - high.astype(F32)).astype(BF16)


def mm(a, b):
    return jnp.dot(a, b, preferred_element_type=F32)


def mm_nt(a, b):
    return lax.dot_general(a, b, (((1,), (1,)), ((), ())), preferred_element_type=F32)


def spread_nodes():
    r, j = iota((NP, 256), 0), iota((NP, 256), 1)
    body = r < BODY
    high = (body & ((j == r) | (j == r + BODY))) | (~body & ((j == r + 160) | (j == r + 164)))
    low = (body & (j == r + 2 * BODY)) | (~body & (j == r + 168))
    return ones_where(high), ones_where(low)


def stack_state(q_ref):
    columns = []
    for f in range(4):
        high, low = halves(q_ref[f, 0:BODY, :])
        tail = q_ref[f, BODY:NR, :]
        tail_high = tail.astype(BF16).astype(F32)
        tail_low = pltpu.roll(tail - tail_high, 4, 0)
        tails = jnp.concatenate([tail_high + tail_low, tail_high], axis=0).astype(BF16)
        columns.append(jnp.concatenate([high, low, high, tails], axis=0))
    return jnp.concatenate(columns, axis=1)


def kernel(
    n_group,
    n_sub,
    fields_hbm,
    diff_hbm,
    interp_hbm,
    lift_hbm,
    jac_hbm,
    scale_hbm,
    angle_hbm,
    reflect_hbm,
    send_hbm,
    recv_hbm,
    class_hbm,
    out_ref,
    fields,
    diff,
    interp,
    lift,
    jac,
    scale,
    angle,
    reflect,
    send,
    recv,
    klass,
    q,
    res,
    st,
    fpad,
    w_face,
    w_diff,
    w_lift,
    sel,
    oh_local,
    oh_far,
    coef,
    jcoef,
    w_fl,
    e_sel,
    oh_sent,
    sent_coef,
    sent_flux,
    sent_face,
    base,
    own,
    table,
    send_buf,
    recv_buf,
    load_sem,
    send_sem,
    recv_sem,
):
    g, s = lax.axis_index("group"), lax.axis_index("sub")
    g_next, g_prev = lax.rem(g + 1, n_group), lax.rem(g + n_group - 1, n_group)
    s_next, s_prev = lax.rem(s + 1, n_sub), lax.rem(s + n_sub - 1, n_sub)
    exists = (s < n_sub - 1, s > 0, g < n_group - 1, g > 0)
    peers = ((g, s_next), (g, s_prev), (g_next, s), (g_prev, s))

    loads = [
        pltpu.make_async_copy(src, dst, load_sem.at[i])
        for i, (src, dst) in enumerate(
            (
                (interp_hbm, interp),
                (fields_hbm, fields),
                (send_hbm, send),
                (recv_hbm, recv),
                (class_hbm, klass),
                (angle_hbm, angle),
                (scale_hbm, scale),
                (reflect_hbm, reflect),
                (jac_hbm, jac),
                (diff_hbm, diff),
                (lift_hbm, lift),
            )
        )
    ]
    for load in loads:
        load.start()
    recv_buf[...] = jnp.zeros_like(recv_buf)
    barrier = pltpu.get_barrier_semaphore()
    for peer, there in zip(peers, exists):

        @pl.when(there)
        def _(peer=peer):
            pl.semaphore_signal(barrier, inc=1, device_id=peer, device_id_type=MESH)


    spread_high, spread_low = spread_nodes()
    fpad[...] = jnp.zeros_like(fpad)
    loads[0].wait()
    rows = jnp.transpose(interp[...], (1, 0))
    for k in range(4):
        fpad[k * FR : k * FR + NFP, :] = rows[k * NFP : (k + 1) * NFP, :]
    high, low = halves(fpad[...])
    w_face[...] = (mm(high, spread_high) + mm(low, spread_low)).astype(BF16)
    loads[1].wait()
    for f in range(4):
        q[f, BODY:NR, :] = jnp.zeros((NR - BODY, ELEM), F32)
        q[f, 0:NP, :] = fields[pl.ds(f, NP, stride=4), :]
    loads[2].wait()
    for j in range(4):
        wanted = jnp.transpose(jnp.broadcast_to(send[j : j + 1, :], (CAP, CAP)), (1, 0))[:, 0:1]
        sel[j * CAP : (j + 1) * CAP, :] = ones_where(iota((CAP, FACES), 1) == wanted)

    def copy_to(m, j):
        return pltpu.make_async_remote_copy(
            src_ref=send_buf.at[m, j],
            dst_ref=recv_buf.at[m, j],
            send_sem=send_sem.at[m, j],
            recv_sem=recv_sem.at[m, j],
            device_id=peers[j],
            device_id_type=MESH,
        )

    def traces_of(state):
        traces = mm(w_face[...], state)
        found, blocks = {}, {}
        for f in range(4):
            for k in range(4):
                found[f, k] = traces[k * FR : (k + 1) * FR, f * ELEM : (f + 1) * ELEM]
                blocks[0, f, k], blocks[1, f, k] = halves(found[f, k])
        whole = jnp.concatenate(
            [
                jnp.concatenate([blocks[h, f, k] for k in range(4)], axis=1)
                for h in range(2)
                for f in POS
            ],
            axis=0,
        )
        return found, whole

    def keep(state, found, whole):
        st[...] = state
        table[...] = whole
        for f in range(4):
            for k in range(4):
                own[f, k] = found[f, k]

    def pack(whole):
        packed = mm_nt(sel[...], whole)
        return packed[:, 0:128] + packed[:, 128:256]

    def send_rows(m, rows):
        for j in range(4):
            send_buf[m, j] = rows[j * CAP : (j + 1) * CAP, :]

    def launch(m):
        for j in (2, 3, 0, 1):

            @pl.when(exists[j])
            def _(j=j):
                copy_to(m, j).start()


    def c8(i, k):
        return coef[i, k][None]

    def tile(x):
        return x.reshape(FR // 8, 8, ELEM)

    def rows_of(array, f, k):
        return tile(array[POS[f] * FR : (POS[f] + 1) * FR, k * ELEM : (k + 1) * ELEM])

    def lift_up(ups):
        parts = {}
        for k in range(4):
            nx, ny, nz = (c8(i, k) for i in range(3))
            up = ups[k]
            for f, term in enumerate((up, nx * up, ny * up, nz * up)):
                parts[0, k, f], parts[1, k, f] = halves(term.reshape(FR, ELEM))
        flux = jnp.concatenate(
            [
                jnp.concatenate([parts[h, k, f] for f in range(4)], axis=1)
                for h in range(2)
                for k in range(4)
            ],
            axis=0,
        )
        lifted = mm(w_lift[...], flux)
        return lifted[0:NR, :] + lifted[NR : 2 * NR, :]

    def local_part(a_now, b_now):
        change = [None] * 4
        vol = None
        for a in range(3):
            slopes = mm(w_diff[a], st[:, ELEM : 4 * ELEM])
            for c in range(3):
                term = slopes[:, c * ELEM : (c + 1) * ELEM].reshape(NR // 8, 8, ELEM) * jcoef[a, c][None]
                vol = term if vol is None else vol + term
        change[0] = a_now * res[0] + vol.reshape(NR, ELEM)
        slopes = [mm(w_diff[a], st[:, 0:ELEM]).reshape(NR // 8, 8, ELEM) for a in range(3)]
        for c in range(3):
            vol = sum(slopes[a] * jcoef[a, c][None] for a in range(3))
            change[1 + c] = a_now * res[1 + c] + vol.reshape(NR, ELEM)
        near = mm(table[...], oh_local[...])
        near = near[0:128, :] + near[128:256, :]
        ups = []
        for k in range(4):
            po, uo, vo, wo = (tile(own[f, k]) for f in range(4))
            pn, un, vn, wn = (rows_of(near, f, k) for f in range(4))
            nx, ny, nz, sc, rf = (c8(i, k) for i in range(5))
            minus = nx * uo + ny * vo + nz * wo
            got = pn + (nx * un + ny * vn + nz * wn)
            ups.append(sc * (got + rf * (po - minus) - (po + minus)))
        lifted = lift_up(ups)
        for f in range(4):
            new = change[f] + lifted[:, f * ELEM : (f + 1) * ELEM]
            res[f] = new
            q[f] = q[f] + b_now * new

    def received(m):
        arrived = recv_buf[m].reshape(SLOTS, 128)
        high = arrived.astype(BF16).astype(F32)
        both = jnp.concatenate([high, arrived - high], axis=0)
        return jnp.transpose(both, (1, 0)).astype(BF16)

    def far_part(m, b_now):
        far = mm(received(m), oh_far[...])
        ups = []
        for k in range(4):
            pn, un, vn, wn = (rows_of(far, f, k) for f in range(4))
            nx, ny, nz, sc = (c8(i, k) for i in range(4))
            ups.append(sc * (pn + (nx * un + ny * vn + nz * wn)))
        lifted = lift_up(ups)
        for f in range(4):
            more = lifted[:, f * ELEM : (f + 1) * ELEM]
            res[f] = res[f] + more
            q[f] = q[f] + b_now * more

    def answer(m, b_now):
        far = mm(received(m), oh_sent[...])
        parts = {}
        for k in range(4):
            terms = [rows_of(far, f, k) * sent_coef[f, k][None] for f in range(4)]
            up = (terms[0] + terms[1]) + (terms[2] + terms[3])
            for p in range(2):
                parts[0, k, p], parts[1, k, p] = halves((up * sent_flux[p, k][None]).reshape(FR, ELEM))
        flux = jnp.concatenate(
            [
                jnp.concatenate([parts[h, k, p] for p in range(2)], axis=1)
                for h in (0, 1, 0)
                for k in range(4)
            ],
            axis=0,
        )
        moved = mm(w_fl[...], flux)
        kept = []
        for p in range(2):
            kept.append(
                sum(
                    tile(moved[k * FR : (k + 1) * FR, p * ELEM : (p + 1) * ELEM]) * sent_face[k][None]
                    for k in range(4)
                ).reshape(FR, ELEM)
            )
        turned = jnp.transpose(jnp.concatenate(kept + kept, axis=0), (1, 0))
        turned = jnp.where(iota((SLOTS, 128), 1) < SLOTS, turned[0:SLOTS, :], turned[SLOTS : 2 * SLOTS, :])
        send_rows(m + 1, base[...] + b_now * turned)

    state = stack_state(q)
    found, whole = traces_of(state)
    send_rows(0, pack(whole))
    keep(state, found, whole)
    pl.semaphore_wait(barrier, sum(e.astype(jnp.int32) for e in exists))
    launch(0)

    for load in loads[3:]:
        load.wait()
    for k in range(4):
        rows = slice(k * ELEM, (k + 1) * ELEM)
        where = jnp.where(klass[k : k + 1, :] == 0, recv[k : k + 1, :], -1)
        oh_local[:, rows] = ones_where(iota((FACES, ELEM), 0) == where)
        slot = iota((2 * SLOTS, ELEM), 0)
        slot = jnp.where(slot >= SLOTS, slot - SLOTS, slot)
        oh_far[:, rows] = ones_where(slot + FACES == where)
        first, second = angle[0, k : k + 1, :], angle[1, k : k + 1, :]
        flat = jnp.cos(second)
        kinds = klass[k : k + 1, :]
        mirror = jnp.zeros((1, ELEM), F32)
        for c in range(4):
            mirror = mirror + jnp.where(kinds == c + 1, reflect[c], 0.0)
        for i, row in enumerate(
            (
                -(jnp.cos(first) * flat),
                -(jnp.sin(first) * flat),
                -jnp.sin(second),
                0.5 * scale[k : k + 1, :],
                mirror,
            )
        ):
            coef[i, k] = jnp.broadcast_to(row, (8, ELEM))
    for a in range(3):
        high, low = halves(diff[a] * (-DT))
        w_diff[a] = jnp.zeros((NR, 256), BF16)
        w_diff[a, 0:NP, :] = (mm(high, spread_high) + mm(low, spread_low)).astype(BF16)
        for c in range(3):
            jcoef[a, c] = jnp.broadcast_to(jac[a, c : c + 1, :], (8, ELEM))
    r, j = iota((4 * NFP, 4 * FR), 0), iota((4 * NFP, 4 * FR), 1)
    face = (r >= NFP).astype(jnp.int32) + (r >= 2 * NFP).astype(jnp.int32) + (r >= 3 * NFP).astype(jnp.int32)
    spread_face = ones_where(j == r + (FR - NFP) * face)
    high, low = halves(lift[...] * DT)
    high, low = mm(high, spread_face).astype(BF16), mm(low, spread_face).astype(BF16)
    w_lift[...] = jnp.zeros_like(w_lift)
    w_lift[0:NP, 0:128] = high
    w_lift[0:NP, 128:256] = high
    w_lift[NR : NR + NP, 0:128] = low
    f_high, f_low = halves(fpad[...])
    both = mm(f_high, high) + (mm(f_high, low) + mm(f_low, high))
    high, low = halves(both)
    w_fl[:, 0:128] = high
    w_fl[:, 128:256] = high
    w_fl[:, 256:384] = low
    picked = [sel[:, k * ELEM : (k + 1) * ELEM] for k in range(4)]
    element = sum(x.astype(F32) for x in picked).astype(BF16)
    e_sel[0:SLOTS, :] = element
    e_sel[SLOTS : 2 * SLOTS, :] = element
    upper = iota((8, ELEM), 1) < SLOTS
    for k in range(4):
        rows = slice(k * ELEM, (k + 1) * ELEM)
        oh_sent[:, rows] = mm_nt(oh_far[:, rows], e_sel[...]).astype(BF16)
        twice = jnp.concatenate([picked[k], picked[k]], axis=0)
        sent_face[k] = mm_nt(jnp.ones((8, ELEM), BF16), twice)
        nx, ny, nz, sc = (coef[i, k] for i in range(4))
        high, low = halves(jnp.concatenate([nx, ny, nz, sc], axis=0))
        there = mm_nt(high, e_sel[...]) + mm_nt(low, e_sel[...])
        nx, ny, nz, sc = (there[i * 8 : (i + 1) * 8, :] for i in range(4))
        for f, term in enumerate((sc, sc * nx, sc * ny, sc * nz)):
            sent_coef[f, k] = term
        sent_flux[0, k] = jnp.where(upper, 1.0, nx)
        sent_flux[1, k] = jnp.where(upper, ny, nz)
    for f in range(4):
        res[f] = jnp.zeros((NR, ELEM), F32)

    def arrive(m):
        for j in (0, 1, 2, 3):

            @pl.when(exists[j ^ 1])
            def _(j=j):
                copy_to(m, j).wait_recv()

    def pick_of(values, m):
        out = jnp.float32(values[0])
        for i in range(1, SECTIONS):
            out = jnp.where(m == i, jnp.float32(values[i]), out)
        return out

    def section(m, carry):
        a_now, b_now = pick_of(RK_A, m), pick_of(RK_B, m)
        local_part(a_now, b_now)
        base[...] = pack(traces_of(stack_state(q))[1])
        arrive(m)
        answer(m, b_now)
        launch(m + 1)
        far_part(m, b_now)
        state = stack_state(q)
        keep(state, *traces_of(state))
        return carry

    lax.fori_loop(0, SECTIONS - 1, section, 0)
    local_part(RK_A[-1], RK_B[-1])
    arrive(SECTIONS - 1)
    far_part(SECTIONS - 1, RK_B[-1])
    for j in range(4):

        @pl.when(exists[j])
        def _(j=j):
            for m in range(SECTIONS):
                copy_to(m, j).wait_send()

    for f in range(4):
        out_ref[pl.ds(f, NP, stride=4), :] = q[f, 0:NP, :]


def hand_on(x_ref, out_ref, sem):
    copy = pltpu.make_async_copy(x_ref, out_ref, sem)
    copy.start()
    copy.wait()


def shards(n_group, n_sub, fields, diff_ops, face_interp, *rest):
    rows = jnp.transpose(fields, (1, 0, 2)).reshape(4 * NP, ELEM)
    args = (rows, diff_ops, jnp.transpose(face_interp, (1, 0))) + rest
    vm = pltpu.VMEM
    loaded = [
        pltpu.SMEM(x.shape, x.dtype) if i == 7 else vm(x.shape, x.dtype) for i, x in enumerate(args)
    ]
    args = tuple(pltpu.with_memory_space_constraint(x, pltpu.HBM) for x in args)
    out = pl.pallas_call(
        functools.partial(kernel, n_group, n_sub),
        out_shape=jax.ShapeDtypeStruct(rows.shape, F32),
        in_specs=[pl.BlockSpec(memory_space=pl.ANY)] * len(args),
        out_specs=pl.BlockSpec(memory_space=pltpu.VMEM),
        scratch_shapes=loaded
        + [
            vm((4, NR, ELEM), F32),
            vm((4, NR, ELEM), F32),
            vm((256, FACES), BF16),
            vm((4 * FR, NP), F32),
            vm((4 * FR, 256), BF16),
            vm((3, NR, 256), BF16),
            vm((2 * NR, 256), BF16),
            vm((SLOTS, FACES), BF16),
            vm((FACES, FACES), BF16),
            vm((2 * SLOTS, FACES), BF16),
            vm((5, 4, 8, ELEM), F32),
            vm((3, 3, 8, ELEM), F32),
            vm((4 * FR, 3 * 4 * FR), BF16),
            vm((2 * SLOTS, ELEM), BF16),
            vm((2 * SLOTS, FACES), BF16),
            vm((4, 4, 8, ELEM), F32),
            vm((2, 4, 8, ELEM), F32),
            vm((4, 8, ELEM), F32),
            vm((SLOTS, 128), F32),
            vm((4, 4, FR, ELEM), F32),
            vm((256, FACES), BF16),
            vm((SECTIONS, 4, CAP, 128), F32),
            vm((SECTIONS, 4, CAP, 128), F32),
            pltpu.SemaphoreType.DMA((len(args),)),
            pltpu.SemaphoreType.DMA((SECTIONS, 4)),
            pltpu.SemaphoreType.DMA((SECTIONS, 4)),
        ],
        compiler_params=pltpu.CompilerParams(
            collective_id=0, has_side_effects=True, vmem_limit_bytes=16 << 20
        ),
        name="sections",
    )(*args)
    out = pl.pallas_call(
        hand_on,
        out_shape=jax.ShapeDtypeStruct(out.shape, F32),
        in_specs=[pl.BlockSpec(memory_space=pltpu.VMEM)],
        out_specs=pl.BlockSpec(memory_space=pl.ANY),
        scratch_shapes=[pltpu.SemaphoreType.DMA],
        compiler_params=pltpu.CompilerParams(vmem_limit_bytes=8 << 20),
        name="hand_on",
    )(out)
    return jnp.transpose(out.reshape(NP, 4, ELEM), (1, 0, 2))


def solution(mesh):
    both = ("group", "sub")
    return jax.shard_map(
        functools.partial(shards, mesh.shape["group"], mesh.shape["sub"]),
        mesh=mesh,
        in_specs=(
            P(None, None, both),
            P(),
            P(),
            P(),
            P(None, None, both),
            P(None, both),
            P(None, None, both),
            P(),
            P(None, both),
            P(None, both),
            P(None, both),
        ),
        out_specs=P(None, None, both),
        check_vma=False,
    )
```

```python
import functools

import jax
import jax.numpy as jnp
from jax import lax
from jax.experimental import pallas as pl
from jax.experimental.pallas import tpu as pltpu
from jax.sharding import PartitionSpec as P

MESH = pl.DeviceIdType.MESH
F32 = jnp.float32
BF16 = jnp.bfloat16
RK_A = (
    0.0,
    -567301805773.0 / 1357537059087.0,
    -2404267990393.0 / 2016746695238.0,
    -3550918686646.0 / 2091501179385.0,
    -1275806237668.0 / 842570457699.0,
)
RK_B = (
    1432997174477.0 / 9575080441755.0,
    5161836677717.0 / 13612068292357.0,
    1720146321549.0 / 2090206949498.0,
    3134564353537.0 / 4481467310338.0,
    2277821191437.0 / 14882151754819.0,
)
DT = 0.3
SECTIONS = 5
NP = 84
NR = 88
FR = 32
NFP = 28
ELEM = 128
FACES = 4 * ELEM
CAP = 16
SLOTS = 4 * CAP
POS = (0, 2, 1, 3)
BODY = 80


def iota(shape, dim):
    return lax.broadcasted_iota(jnp.int32, shape, dim)


def ones_where(cond):
    return jnp.where(cond, 1.0, 0.0).astype(BF16)


def halves(x):
    high = x.astype(BF16)
    return high, (x - high.astype(F32)).astype(BF16)


def mm(a, b):
    return jnp.dot(a, b, preferred_element_type=F32)


def mm_nt(a, b):
    return lax.dot_general(a, b, (((1,), (1,)), ((), ())), preferred_element_type=F32)


def spread_nodes():
    r, j = iota((NP, 256), 0), iota((NP, 256), 1)
    body = r < BODY
    high = (body & ((j == r) | (j == r + BODY))) | (~body & ((j == r + 160) | (j == r + 164)))
    low = (body & (j == r + 2 * BODY)) | (~body & (j == r + 168))
    return ones_where(high), ones_where(low)


def stack_state(q_ref):
    columns = []
    for f in range(4):
        high, low = halves(q_ref[f, 0:BODY, :])
        tail = q_ref[f, BODY:NR, :]
        tail_high = tail.astype(BF16).astype(F32)
        tail_low = pltpu.roll(tail - tail_high, 4, 0)
        tails = jnp.concatenate([tail_high + tail_low, tail_high], axis=0).astype(BF16)
        columns.append(jnp.concatenate([high, low, high, tails], axis=0))
    return jnp.concatenate(columns, axis=1)


def kernel(
    n_group,
    n_sub,
    fields_hbm,
    diff_hbm,
    interp_hbm,
    lift_hbm,
    jac_hbm,
    scale_hbm,
    angle_hbm,
    reflect_hbm,
    send_hbm,
    recv_hbm,
    class_hbm,
    out_ref,
    fields,
    diff,
    interp,
    lift,
    jac,
    scale,
    angle,
    reflect,
    send,
    recv,
    klass,
    q,
    res,
    st,
    fpad,
    w_face,
    w_diff,
    w_lift,
    sel,
    oh_local,
    oh_far,
    coef,
    jcoef,
    w_fl,
    e_sel,
    oh_sent,
    sent_coef,
    sent_flux,
    sent_face,
    base,
    own,
    table,
    send_buf,
    recv_buf,
    load_sem,
    send_sem,
    recv_sem,
):
    g, s = lax.axis_index("group"), lax.axis_index("sub")
    g_next, g_prev = lax.rem(g + 1, n_group), lax.rem(g + n_group - 1, n_group)
    s_next, s_prev = lax.rem(s + 1, n_sub), lax.rem(s + n_sub - 1, n_sub)
    exists = (s < n_sub - 1, s > 0, g < n_group - 1, g > 0)
    peers = ((g, s_next), (g, s_prev), (g_next, s), (g_prev, s))

    loads = [
        pltpu.make_async_copy(src, dst, load_sem.at[i])
        for i, (src, dst) in enumerate(
            (
                (interp_hbm, interp),
                (fields_hbm, fields),
                (send_hbm, send),
                (recv_hbm, recv),
                (class_hbm, klass),
                (angle_hbm, angle),
                (scale_hbm, scale),
                (reflect_hbm, reflect),
                (jac_hbm, jac),
                (diff_hbm, diff),
                (lift_hbm, lift),
            )
        )
    ]
    barrier = pltpu.get_barrier_semaphore()
    for peer, there in zip(peers, exists):

        @pl.when(there)
        def _(peer=peer):
            pl.semaphore_signal(barrier, inc=1, device_id=peer, device_id_type=MESH)

    for load in loads:
        load.start()
    for j in range(4):

        @pl.when(jnp.logical_not(exists[j ^ 1]))
        def _(j=j):
            for m in range(SECTIONS):
                recv_buf[m, j] = jnp.zeros((CAP, 128), F32)

    spread_high, spread_low = spread_nodes()
    fpad[...] = jnp.zeros_like(fpad)
    loads[0].wait()
    rows = jnp.transpose(interp[...], (1, 0))
    for k in range(4):
        fpad[k * FR : k * FR + NFP, :] = rows[k * NFP : (k + 1) * NFP, :]
    high, low = halves(fpad[...])
    w_face[...] = (mm(high, spread_high) + mm(low, spread_low)).astype(BF16)
    loads[1].wait()
    for f in range(4):
        q[f, BODY:NR, :] = jnp.zeros((NR - BODY, ELEM), F32)
        q[f, 0:NP, :] = fields[pl.ds(f, NP, stride=4), :]
    loads[2].wait()
    for j in range(4):
        wanted = jnp.transpose(jnp.broadcast_to(send[j : j + 1, :], (CAP, CAP)), (1, 0))[:, 0:1]
        sel[j * CAP : (j + 1) * CAP, :] = ones_where(iota((CAP, FACES), 1) == wanted)

    def copy_to(m, j):
        return pltpu.make_async_remote_copy(
            src_ref=send_buf.at[m, j],
            dst_ref=recv_buf.at[m, j],
            send_sem=send_sem.at[j],
            recv_sem=recv_sem.at[m, j],
            device_id=peers[j],
            device_id_type=MESH,
        )

    def traces_of(state):
        traces = mm(w_face[...], state)
        found, blocks = {}, {}
        for f in range(4):
            for k in range(4):
                found[f, k] = traces[k * FR : (k + 1) * FR, f * ELEM : (f + 1) * ELEM]
                blocks[0, f, k], blocks[1, f, k] = halves(found[f, k])
        whole = jnp.concatenate(
            [
                jnp.concatenate([blocks[h, f, k] for k in range(4)], axis=1)
                for h in range(2)
                for f in POS
            ],
            axis=0,
        )
        return found, whole

    def keep(state, found, whole):
        st[...] = state
        table[...] = whole
        for f in range(4):
            for k in range(4):
                own[f, k] = found[f, k]

    def pack(whole):
        packed = mm_nt(sel[...], whole)
        return packed[:, 0:128] + packed[:, 128:256]

    def send_rows(m, rows):
        for j in range(4):
            send_buf[m, j] = rows[j * CAP : (j + 1) * CAP, :]

    def launch(m):
        for j in (0, 1, 2, 3):

            @pl.when(exists[j])
            def _(j=j):
                copy_to(m, j).start()


    def c8(i, k):
        return coef[i, k][None]

    def tile(x):
        return x.reshape(FR // 8, 8, ELEM)

    def rows_of(array, f, k):
        return tile(array[POS[f] * FR : (POS[f] + 1) * FR, k * ELEM : (k + 1) * ELEM])

    def lift_up(ups):
        parts = {}
        for k in range(4):
            nx, ny, nz = (c8(i, k) for i in range(3))
            up = ups[k]
            for f, term in enumerate((up, nx * up, ny * up, nz * up)):
                parts[0, k, f], parts[1, k, f] = halves(term.reshape(FR, ELEM))
        flux = jnp.concatenate(
            [
                jnp.concatenate([parts[h, k, f] for f in range(4)], axis=1)
                for h in range(2)
                for k in range(4)
            ],
            axis=0,
        )
        lifted = mm(w_lift[...], flux)
        return lifted[0:NR, :] + lifted[NR : 2 * NR, :]

    def local_part(a_now, b_now):
        change = [None] * 4
        vol = None
        for a in range(3):
            slopes = mm(w_diff[a], st[:, ELEM : 4 * ELEM])
            for c in range(3):
                term = slopes[:, c * ELEM : (c + 1) * ELEM].reshape(NR // 8, 8, ELEM) * jcoef[a, c][None]
                vol = term if vol is None else vol + term
        change[0] = a_now * res[0] + vol.reshape(NR, ELEM)
        slopes = [mm(w_diff[a], st[:, 0:ELEM]).reshape(NR // 8, 8, ELEM) for a in range(3)]
        for c in range(3):
            vol = sum(slopes[a] * jcoef[a, c][None] for a in range(3))
            change[1 + c] = a_now * res[1 + c] + vol.reshape(NR, ELEM)
        near = mm(table[...], oh_local[...])
        near = near[0:128, :] + near[128:256, :]
        ups = []
        for k in range(4):
            po, uo, vo, wo = (tile(own[f, k]) for f in range(4))
            pn, un, vn, wn = (rows_of(near, f, k) for f in range(4))
            nx, ny, nz, sc, rf = (c8(i, k) for i in range(5))
            minus = nx * uo + ny * vo + nz * wo
            got = pn + (nx * un + ny * vn + nz * wn)
            ups.append(sc * (got + rf * (po - minus) - (po + minus)))
        lifted = lift_up(ups)
        for f in range(4):
            new = change[f] + lifted[:, f * ELEM : (f + 1) * ELEM]
            res[f] = new
            q[f] = q[f] + b_now * new

    def received(m):
        arrived = recv_buf[m].reshape(SLOTS, 128)
        high = arrived.astype(BF16).astype(F32)
        both = jnp.concatenate([high, arrived - high], axis=0)
        return jnp.transpose(both, (1, 0)).astype(BF16)

    def far_part(m, b_now):
        far = mm(received(m), oh_far[...])
        ups = []
        for k in range(4):
            pn, un, vn, wn = (rows_of(far, f, k) for f in range(4))
            nx, ny, nz, sc = (c8(i, k) for i in range(4))
            ups.append(sc * (pn + (nx * un + ny * vn + nz * wn)))
        lifted = lift_up(ups)
        for f in range(4):
            more = lifted[:, f * ELEM : (f + 1) * ELEM]
            res[f] = res[f] + more
            q[f] = q[f] + b_now * more

    def answer(m, b_now):
        far = mm(received(m), oh_sent[...])
        parts = {}
        for k in range(4):
            terms = [rows_of(far, f, k) * sent_coef[f, k][None] for f in range(4)]
            up = (terms[0] + terms[1]) + (terms[2] + terms[3])
            for p in range(2):
                parts[0, k, p], parts[1, k, p] = halves((up * sent_flux[p, k][None]).reshape(FR, ELEM))
        flux = jnp.concatenate(
            [
                jnp.concatenate([parts[h, k, p] for p in range(2)], axis=1)
                for h in (0, 1, 0)
                for k in range(4)
            ],
            axis=0,
        )
        moved = mm(w_fl[...], flux)
        kept = []
        for p in range(2):
            kept.append(
                sum(
                    tile(moved[k * FR : (k + 1) * FR, p * ELEM : (p + 1) * ELEM]) * sent_face[k][None]
                    for k in range(4)
                ).reshape(FR, ELEM)
            )
        turned = jnp.transpose(jnp.concatenate(kept + kept, axis=0), (1, 0))
        turned = jnp.where(iota((SLOTS, 128), 1) < SLOTS, turned[0:SLOTS, :], turned[SLOTS : 2 * SLOTS, :])
        send_rows(m + 1, base[...] + b_now * turned)

    state = stack_state(q)
    found, whole = traces_of(state)
    send_rows(0, pack(whole))
    keep(state, found, whole)
    pl.semaphore_wait(barrier, sum(e.astype(jnp.int32) for e in exists))
    launch(0)

    for load in loads[3:]:
        load.wait()
    for k in range(4):
        rows = slice(k * ELEM, (k + 1) * ELEM)
        where = jnp.where(klass[k : k + 1, :] == 0, recv[k : k + 1, :], -1)
        oh_local[:, rows] = ones_where(iota((FACES, ELEM), 0) == where)
        slot = iota((2 * SLOTS, ELEM), 0)
        slot = jnp.where(slot >= SLOTS, slot - SLOTS, slot)
        oh_far[:, rows] = ones_where(slot + FACES == where)
        first, second = angle[0, k : k + 1, :], angle[1, k : k + 1, :]
        flat = jnp.cos(second)
        kinds = klass[k : k + 1, :]
        mirror = jnp.zeros((1, ELEM), F32)
        for c in range(4):
            mirror = mirror + jnp.where(kinds == c + 1, reflect[c], 0.0)
        for i, row in enumerate(
            (
                -(jnp.cos(first) * flat),
                -(jnp.sin(first) * flat),
                -jnp.sin(second),
                0.5 * scale[k : k + 1, :],
                mirror,
            )
        ):
            coef[i, k] = jnp.broadcast_to(row, (8, ELEM))
    for a in range(3):
        high, low = halves(diff[a] * (-DT))
        w_diff[a] = jnp.zeros((NR, 256), BF16)
        w_diff[a, 0:NP, :] = (mm(high, spread_high) + mm(low, spread_low)).astype(BF16)
        for c in range(3):
            jcoef[a, c] = jnp.broadcast_to(jac[a, c : c + 1, :], (8, ELEM))
    r, j = iota((4 * NFP, 4 * FR), 0), iota((4 * NFP, 4 * FR), 1)
    face = (r >= NFP).astype(jnp.int32) + (r >= 2 * NFP).astype(jnp.int32) + (r >= 3 * NFP).astype(jnp.int32)
    spread_face = ones_where(j == r + (FR - NFP) * face)
    high, low = halves(lift[...] * DT)
    high, low = mm(high, spread_face).astype(BF16), mm(low, spread_face).astype(BF16)
    w_lift[...] = jnp.zeros_like(w_lift)
    w_lift[0:NP, 0:128] = high
    w_lift[0:NP, 128:256] = high
    w_lift[NR : NR + NP, 0:128] = low
    f_high, f_low = halves(fpad[...])
    both = mm(f_high, high) + (mm(f_high, low) + mm(f_low, high))
    high, low = halves(both)
    w_fl[:, 0:128] = high
    w_fl[:, 128:256] = high
    w_fl[:, 256:384] = low
    picked = [sel[:, k * ELEM : (k + 1) * ELEM] for k in range(4)]
    element = sum(x.astype(F32) for x in picked).astype(BF16)
    e_sel[0:SLOTS, :] = element
    e_sel[SLOTS : 2 * SLOTS, :] = element
    upper = iota((8, ELEM), 1) < SLOTS
    for k in range(4):
        rows = slice(k * ELEM, (k + 1) * ELEM)
        oh_sent[:, rows] = mm_nt(oh_far[:, rows], e_sel[...]).astype(BF16)
        twice = jnp.concatenate([picked[k], picked[k]], axis=0)
        sent_face[k] = mm_nt(jnp.ones((8, ELEM), BF16), twice)
        nx, ny, nz, sc = (coef[i, k] for i in range(4))
        high, low = halves(jnp.concatenate([nx, ny, nz, sc], axis=0))
        there = mm_nt(high, e_sel[...]) + mm_nt(low, e_sel[...])
        nx, ny, nz, sc = (there[i * 8 : (i + 1) * 8, :] for i in range(4))
        for f, term in enumerate((sc, sc * nx, sc * ny, sc * nz)):
            sent_coef[f, k] = term
        sent_flux[0, k] = jnp.where(upper, 1.0, nx)
        sent_flux[1, k] = jnp.where(upper, ny, nz)
    for f in range(4):
        res[f] = jnp.zeros((NR, ELEM), F32)

    def arrive(m):
        for j in (0, 1, 2, 3):

            @pl.when(exists[j ^ 1])
            def _(j=j):
                copy_to(m, j).wait_recv()

    def sent(m):
        for j in (0, 1, 2, 3):

            @pl.when(exists[j])
            def _(j=j):
                copy_to(m, j).wait_send()

    def pick_of(values, m):
        out = jnp.float32(values[0])
        for i in range(1, SECTIONS):
            out = jnp.where(m == i, jnp.float32(values[i]), out)
        return out

    def section(m, carry):
        a_now, b_now = pick_of(RK_A, m), pick_of(RK_B, m)
        local_part(a_now, b_now)
        base[...] = pack(traces_of(stack_state(q))[1])
        sent(m)
        arrive(m)
        answer(m, b_now)
        launch(m + 1)
        far_part(m, b_now)
        state = stack_state(q)
        keep(state, *traces_of(state))
        return carry

    lax.fori_loop(0, SECTIONS - 1, section, 0)
    local_part(RK_A[-1], RK_B[-1])
    sent(SECTIONS - 1)
    arrive(SECTIONS - 1)
    far_part(SECTIONS - 1, RK_B[-1])
    for f in range(4):
        out_ref[pl.ds(f, NP, stride=4), :] = q[f, 0:NP, :]


def hand_on(x_ref, out_ref, sem):
    copy = pltpu.make_async_copy(x_ref, out_ref, sem)
    copy.start()
    copy.wait()


def shards(n_group, n_sub, fields, diff_ops, face_interp, *rest):
    rows = jnp.transpose(fields, (1, 0, 2)).reshape(4 * NP, ELEM)
    args = (rows, diff_ops, jnp.transpose(face_interp, (1, 0))) + rest
    vm = pltpu.VMEM
    loaded = [
        pltpu.SMEM(x.shape, x.dtype) if i == 7 else vm(x.shape, x.dtype) for i, x in enumerate(args)
    ]
    args = tuple(pltpu.with_memory_space_constraint(x, pltpu.HBM) for x in args)
    out = pl.pallas_call(
        functools.partial(kernel, n_group, n_sub),
        out_shape=jax.ShapeDtypeStruct(rows.shape, F32),
        in_specs=[pl.BlockSpec(memory_space=pl.ANY)] * len(args),
        out_specs=pl.BlockSpec(memory_space=pltpu.VMEM),
        scratch_shapes=loaded
        + [
            vm((4, NR, ELEM), F32),
            vm((4, NR, ELEM), F32),
            vm((256, FACES), BF16),
            vm((4 * FR, NP), F32),
            vm((4 * FR, 256), BF16),
            vm((3, NR, 256), BF16),
            vm((2 * NR, 256), BF16),
            vm((SLOTS, FACES), BF16),
            vm((FACES, FACES), BF16),
            vm((2 * SLOTS, FACES), BF16),
            vm((5, 4, 8, ELEM), F32),
            vm((3, 3, 8, ELEM), F32),
            vm((4 * FR, 3 * 4 * FR), BF16),
            vm((2 * SLOTS, ELEM), BF16),
            vm((2 * SLOTS, FACES), BF16),
            vm((4, 4, 8, ELEM), F32),
            vm((2, 4, 8, ELEM), F32),
            vm((4, 8, ELEM), F32),
            vm((SLOTS, 128), F32),
            vm((4, 4, FR, ELEM), F32),
            vm((256, FACES), BF16),
            vm((SECTIONS, 4, CAP, 128), F32),
            vm((SECTIONS, 4, CAP, 128), F32),
            pltpu.SemaphoreType.DMA((len(args),)),
            pltpu.SemaphoreType.DMA((4,)),
            pltpu.SemaphoreType.DMA((SECTIONS, 4)),
        ],
        compiler_params=pltpu.CompilerParams(
            collective_id=0, has_side_effects=True, vmem_limit_bytes=16 << 20
        ),
        name="sections",
    )(*args)
    out = pl.pallas_call(
        hand_on,
        out_shape=jax.ShapeDtypeStruct(out.shape, F32),
        in_specs=[pl.BlockSpec(memory_space=pltpu.VMEM)],
        out_specs=pl.BlockSpec(memory_space=pl.ANY),
        scratch_shapes=[pltpu.SemaphoreType.DMA],
        compiler_params=pltpu.CompilerParams(vmem_limit_bytes=8 << 20),
        name="hand_on",
    )(out)
    return jnp.transpose(out.reshape(NP, 4, ELEM), (1, 0, 2))


def solution(mesh):
    both = ("group", "sub")
    return jax.shard_map(
        functools.partial(shards, mesh.shape["group"], mesh.shape["sub"]),
        mesh=mesh,
        in_specs=(
            P(None, None, both),
            P(),
            P(),
            P(),
            P(None, None, both),
            P(None, both),
            P(None, None, both),
            P(),
            P(None, both),
            P(None, both),
            P(None, both),
        ),
        out_specs=P(None, None, both),
        check_vma=False,
    )
```

```python
import functools

import jax
import jax.numpy as jnp
from jax import lax
from jax.experimental import pallas as pl
from jax.experimental.pallas import tpu as pltpu
from jax.sharding import PartitionSpec as P

MESH = pl.DeviceIdType.MESH
F32 = jnp.float32
BF16 = jnp.bfloat16
RK_A = (
    0.0,
    -567301805773.0 / 1357537059087.0,
    -2404267990393.0 / 2016746695238.0,
    -3550918686646.0 / 2091501179385.0,
    -1275806237668.0 / 842570457699.0,
)
RK_B = (
    1432997174477.0 / 9575080441755.0,
    5161836677717.0 / 13612068292357.0,
    1720146321549.0 / 2090206949498.0,
    3134564353537.0 / 4481467310338.0,
    2277821191437.0 / 14882151754819.0,
)
DT = 0.3
SECTIONS = 5
NP = 84
NR = 88
FR = 32
NFP = 28
ELEM = 128
FACES = 4 * ELEM
CAP = 16
SLOTS = 4 * CAP
POS = (0, 2, 1, 3)
BODY = 80


def iota(shape, dim):
    return lax.broadcasted_iota(jnp.int32, shape, dim)


def ones_where(cond):
    return jnp.where(cond, 1.0, 0.0).astype(BF16)


def halves(x):
    high = x.astype(BF16)
    return high, (x - high.astype(F32)).astype(BF16)


def mm(a, b):
    return jnp.dot(a, b, preferred_element_type=F32)


def mm_nt(a, b):
    return lax.dot_general(a, b, (((1,), (1,)), ((), ())), preferred_element_type=F32)


def spread_nodes():
    r, j = iota((NP, 256), 0), iota((NP, 256), 1)
    body = r < BODY
    high = (body & ((j == r) | (j == r + BODY))) | (~body & ((j == r + 160) | (j == r + 164)))
    low = (body & (j == r + 2 * BODY)) | (~body & (j == r + 168))
    return ones_where(high), ones_where(low)


def stack_state(q_ref):
    columns = []
    for f in range(4):
        high, low = halves(q_ref[f, 0:BODY, :])
        tail = q_ref[f, BODY:NR, :]
        tail_high = tail.astype(BF16).astype(F32)
        tail_low = pltpu.roll(tail - tail_high, 4, 0)
        tails = jnp.concatenate([tail_high + tail_low, tail_high], axis=0).astype(BF16)
        columns.append(jnp.concatenate([high, low, high, tails], axis=0))
    return jnp.concatenate(columns, axis=1)


def kernel(
    n_group,
    n_sub,
    fields_hbm,
    diff_hbm,
    interp_hbm,
    lift_hbm,
    jac_hbm,
    scale_hbm,
    angle_hbm,
    reflect_hbm,
    send_hbm,
    recv_hbm,
    class_hbm,
    out_ref,
    fields,
    diff,
    interp,
    lift,
    jac,
    scale,
    angle,
    reflect,
    send,
    recv,
    klass,
    q,
    res,
    st,
    fpad,
    w_face,
    w_diff,
    w_lift,
    sel,
    oh_local,
    oh_far,
    coef,
    jcoef,
    w_fl,
    e_sel,
    oh_sent,
    sent_coef,
    sent_flux,
    sent_face,
    base,
    own,
    table,
    send_buf,
    recv_buf,
    load_sem,
    send_sem,
    recv_sem,
):
    g, s = lax.axis_index("group"), lax.axis_index("sub")
    g_next, g_prev = lax.rem(g + 1, n_group), lax.rem(g + n_group - 1, n_group)
    s_next, s_prev = lax.rem(s + 1, n_sub), lax.rem(s + n_sub - 1, n_sub)
    exists = (s < n_sub - 1, s > 0, g < n_group - 1, g > 0)
    peers = ((g, s_next), (g, s_prev), (g_next, s), (g_prev, s))

    loads = [
        pltpu.make_async_copy(src, dst, load_sem.at[i])
        for i, (src, dst) in enumerate(
            (
                (interp_hbm, interp),
                (fields_hbm, fields),
                (send_hbm, send),
                (recv_hbm, recv),
                (class_hbm, klass),
                (angle_hbm, angle),
                (scale_hbm, scale),
                (reflect_hbm, reflect),
                (jac_hbm, jac),
                (diff_hbm, diff),
                (lift_hbm, lift),
            )
        )
    ]
    barrier = pltpu.get_barrier_semaphore()
    for peer, there in zip(peers, exists):

        @pl.when(there)
        def _(peer=peer):
            pl.semaphore_signal(barrier, inc=1, device_id=peer, device_id_type=MESH)

    for load in loads:
        load.start()
    for j in range(4):

        @pl.when(jnp.logical_not(exists[j ^ 1]))
        def _(j=j):
            for m in range(SECTIONS):
                recv_buf[m, j] = jnp.zeros((CAP, 128), F32)

    spread_high, spread_low = spread_nodes()
    fpad[...] = jnp.zeros_like(fpad)
    loads[0].wait()
    rows = jnp.transpose(interp[...], (1, 0))
    for k in range(4):
        fpad[k * FR : k * FR + NFP, :] = rows[k * NFP : (k + 1) * NFP, :]
    high, low = halves(fpad[...])
    w_face[...] = (mm(high, spread_high) + mm(low, spread_low)).astype(BF16)
    loads[1].wait()
    for f in range(4):
        q[f, BODY:NR, :] = jnp.zeros((NR - BODY, ELEM), F32)
        q[f, 0:NP, :] = fields[pl.ds(f, NP, stride=4), :]
    loads[2].wait()
    for j in range(4):
        wanted = jnp.transpose(jnp.broadcast_to(send[j : j + 1, :], (CAP, CAP)), (1, 0))[:, 0:1]
        sel[j * CAP : (j + 1) * CAP, :] = ones_where(iota((CAP, FACES), 1) == wanted)

    def copy_to(m, j):
        return pltpu.make_async_remote_copy(
            src_ref=send_buf.at[m, j],
            dst_ref=recv_buf.at[m, j],
            send_sem=send_sem.at[j],
            recv_sem=recv_sem.at[lax.rem(m, 2) if not isinstance(m, int) else m % 2, j],
            device_id=peers[j],
            device_id_type=MESH,
        )

    def traces_of(state):
        traces = mm(w_face[...], state)
        found, blocks = {}, {}
        for f in range(4):
            for k in range(4):
                found[f, k] = traces[k * FR : (k + 1) * FR, f * ELEM : (f + 1) * ELEM]
                blocks[0, f, k], blocks[1, f, k] = halves(found[f, k])
        whole = jnp.concatenate(
            [
                jnp.concatenate([blocks[h, f, k] for k in range(4)], axis=1)
                for h in range(2)
                for f in POS
            ],
            axis=0,
        )
        return found, whole

    def keep(state, found, whole):
        st[...] = state
        table[...] = whole
        for f in range(4):
            for k in range(4):
                own[f, k] = found[f, k]

    def pack(whole):
        packed = mm_nt(sel[...], whole)
        return packed[:, 0:128] + packed[:, 128:256]

    def send_rows(m, rows):
        for j in range(4):
            send_buf[m, j] = rows[j * CAP : (j + 1) * CAP, :]

    def launch(m):
        for j in (0, 1, 2, 3):

            @pl.when(exists[j])
            def _(j=j):
                copy_to(m, j).start()


    def c8(i, k):
        return coef[i, k][None]

    def tile(x):
        return x.reshape(FR // 8, 8, ELEM)

    def rows_of(array, f, k):
        return tile(array[POS[f] * FR : (POS[f] + 1) * FR, k * ELEM : (k + 1) * ELEM])

    def lift_up(ups):
        parts = {}
        for k in range(4):
            nx, ny, nz = (c8(i, k) for i in range(3))
            up = ups[k]
            for f, term in enumerate((up, nx * up, ny * up, nz * up)):
                parts[0, k, f], parts[1, k, f] = halves(term.reshape(FR, ELEM))
        flux = jnp.concatenate(
            [
                jnp.concatenate([parts[h, k, f] for f in range(4)], axis=1)
                for h in range(2)
                for k in range(4)
            ],
            axis=0,
        )
        lifted = mm(w_lift[...], flux)
        return lifted[0:NR, :] + lifted[NR : 2 * NR, :]

    def local_part(a_now, b_now):
        change = [None] * 4
        vol = None
        for a in range(3):
            slopes = mm(w_diff[a], st[:, ELEM : 4 * ELEM])
            for c in range(3):
                term = slopes[:, c * ELEM : (c + 1) * ELEM].reshape(NR // 8, 8, ELEM) * jcoef[a, c][None]
                vol = term if vol is None else vol + term
        change[0] = a_now * res[0] + vol.reshape(NR, ELEM)
        slopes = [mm(w_diff[a], st[:, 0:ELEM]).reshape(NR // 8, 8, ELEM) for a in range(3)]
        for c in range(3):
            vol = sum(slopes[a] * jcoef[a, c][None] for a in range(3))
            change[1 + c] = a_now * res[1 + c] + vol.reshape(NR, ELEM)
        near = mm(table[...], oh_local[...])
        near = near[0:128, :] + near[128:256, :]
        ups = []
        for k in range(4):
            po, uo, vo, wo = (tile(own[f, k]) for f in range(4))
            pn, un, vn, wn = (rows_of(near, f, k) for f in range(4))
            nx, ny, nz, sc, rf = (c8(i, k) for i in range(5))
            minus = nx * uo + ny * vo + nz * wo
            got = pn + (nx * un + ny * vn + nz * wn)
            ups.append(sc * (got + rf * (po - minus) - (po + minus)))
        lifted = lift_up(ups)
        for f in range(4):
            new = change[f] + lifted[:, f * ELEM : (f + 1) * ELEM]
            res[f] = new
            q[f] = q[f] + b_now * new

    def received(m):
        arrived = recv_buf[m].reshape(SLOTS, 128)
        high = arrived.astype(BF16).astype(F32)
        both = jnp.concatenate([high, arrived - high], axis=0)
        return jnp.transpose(both, (1, 0)).astype(BF16)

    def far_part(m, b_now, last=False):
        far = mm(received(m), oh_far[...])
        ups = []
        for k in range(4):
            pn, un, vn, wn = (rows_of(far, f, k) for f in range(4))
            nx, ny, nz, sc = (c8(i, k) for i in range(4))
            ups.append(sc * (pn + (nx * un + ny * vn + nz * wn)))
        lifted = lift_up(ups)
        for f in range(4):
            more = lifted[:, f * ELEM : (f + 1) * ELEM]
            if last:
                out_ref[pl.ds(f, NP, stride=4), :] = q[f, 0:NP, :] + b_now * more[0:NP, :]
                continue
            res[f] = res[f] + more
            q[f] = q[f] + b_now * more

    def answer(m, b_now):
        far = mm(received(m), oh_sent[...])
        parts = {}
        for k in range(4):
            terms = [rows_of(far, f, k) * sent_coef[f, k][None] for f in range(4)]
            up = (terms[0] + terms[1]) + (terms[2] + terms[3])
            for p in range(2):
                parts[0, k, p], parts[1, k, p] = halves((up * sent_flux[p, k][None]).reshape(FR, ELEM))
        flux = jnp.concatenate(
            [
                jnp.concatenate([parts[h, k, p] for p in range(2)], axis=1)
                for h in (0, 1, 0)
                for k in range(4)
            ],
            axis=0,
        )
        moved = mm(w_fl[...], flux)
        kept = []
        for p in range(2):
            kept.append(
                sum(
                    tile(moved[k * FR : (k + 1) * FR, p * ELEM : (p + 1) * ELEM]) * sent_face[k][None]
                    for k in range(4)
                ).reshape(FR, ELEM)
            )
        turned = jnp.transpose(jnp.concatenate(kept + kept, axis=0), (1, 0))
        turned = jnp.where(iota((SLOTS, 128), 1) < SLOTS, turned[0:SLOTS, :], turned[SLOTS : 2 * SLOTS, :])
        send_rows(m + 1, base[...] + b_now * turned)

    state = stack_state(q)
    found, whole = traces_of(state)
    send_rows(0, pack(whole))
    keep(state, found, whole)
    pl.semaphore_wait(barrier, sum(e.astype(jnp.int32) for e in exists))
    launch(0)

    for load in loads[3:]:
        load.wait()
    for k in range(4):
        rows = slice(k * ELEM, (k + 1) * ELEM)
        where = jnp.where(klass[k : k + 1, :] == 0, recv[k : k + 1, :], -1)
        oh_local[:, rows] = ones_where(iota((FACES, ELEM), 0) == where)
        slot = iota((2 * SLOTS, ELEM), 0)
        slot = jnp.where(slot >= SLOTS, slot - SLOTS, slot)
        oh_far[:, rows] = ones_where(slot + FACES == where)
        first, second = angle[0, k : k + 1, :], angle[1, k : k + 1, :]
        flat = jnp.cos(second)
        kinds = klass[k : k + 1, :]
        mirror = jnp.zeros((1, ELEM), F32)
        for c in range(4):
            mirror = mirror + jnp.where(kinds == c + 1, reflect[c], 0.0)
        for i, row in enumerate(
            (
                -(jnp.cos(first) * flat),
                -(jnp.sin(first) * flat),
                -jnp.sin(second),
                0.5 * scale[k : k + 1, :],
                mirror,
            )
        ):
            coef[i, k] = jnp.broadcast_to(row, (8, ELEM))
    for a in range(3):
        high, low = halves(diff[a] * (-DT))
        w_diff[a] = jnp.zeros((NR, 256), BF16)
        w_diff[a, 0:NP, :] = (mm(high, spread_high) + mm(low, spread_low)).astype(BF16)
        for c in range(3):
            jcoef[a, c] = jnp.broadcast_to(jac[a, c : c + 1, :], (8, ELEM))
    r, j = iota((4 * NFP, 4 * FR), 0), iota((4 * NFP, 4 * FR), 1)
    face = (r >= NFP).astype(jnp.int32) + (r >= 2 * NFP).astype(jnp.int32) + (r >= 3 * NFP).astype(jnp.int32)
    spread_face = ones_where(j == r + (FR - NFP) * face)
    high, low = halves(lift[...] * DT)
    high, low = mm(high, spread_face).astype(BF16), mm(low, spread_face).astype(BF16)
    w_lift[...] = jnp.zeros_like(w_lift)
    w_lift[0:NP, 0:128] = high
    w_lift[0:NP, 128:256] = high
    w_lift[NR : NR + NP, 0:128] = low
    f_high, f_low = halves(fpad[...])
    both = mm(f_high, high) + (mm(f_high, low) + mm(f_low, high))
    high, low = halves(both)
    w_fl[:, 0:128] = high
    w_fl[:, 128:256] = high
    w_fl[:, 256:384] = low
    picked = [sel[:, k * ELEM : (k + 1) * ELEM] for k in range(4)]
    element = sum(x.astype(F32) for x in picked).astype(BF16)
    e_sel[0:SLOTS, :] = element
    e_sel[SLOTS : 2 * SLOTS, :] = element
    upper = iota((8, ELEM), 1) < SLOTS
    for k in range(4):
        rows = slice(k * ELEM, (k + 1) * ELEM)
        oh_sent[:, rows] = mm_nt(oh_far[:, rows], e_sel[...]).astype(BF16)
        twice = jnp.concatenate([picked[k], picked[k]], axis=0)
        sent_face[k] = mm_nt(jnp.ones((8, ELEM), BF16), twice)
        nx, ny, nz, sc = (coef[i, k] for i in range(4))
        high, low = halves(jnp.concatenate([nx, ny, nz, sc], axis=0))
        there = mm_nt(high, e_sel[...]) + mm_nt(low, e_sel[...])
        nx, ny, nz, sc = (there[i * 8 : (i + 1) * 8, :] for i in range(4))
        for f, term in enumerate((sc, sc * nx, sc * ny, sc * nz)):
            sent_coef[f, k] = term
        sent_flux[0, k] = jnp.where(upper, 1.0, nx)
        sent_flux[1, k] = jnp.where(upper, ny, nz)
    for f in range(4):
        res[f] = jnp.zeros((NR, ELEM), F32)

    def arrive(m):
        for j in (0, 1, 2, 3):

            @pl.when(exists[j ^ 1])
            def _(j=j):
                copy_to(m, j).wait_recv()

    def sent(m):
        for j in (0, 1, 2, 3):

            @pl.when(exists[j])
            def _(j=j):
                copy_to(m, j).wait_send()

    def pick_of(values, m):
        out = jnp.float32(values[0])
        for i in range(1, SECTIONS):
            out = jnp.where(m == i, jnp.float32(values[i]), out)
        return out

    def section(m, carry):
        a_now, b_now = pick_of(RK_A, m), pick_of(RK_B, m)
        local_part(a_now, b_now)
        base[...] = pack(traces_of(stack_state(q))[1])
        sent(m)
        arrive(m)
        answer(m, b_now)
        launch(m + 1)
        far_part(m, b_now)
        state = stack_state(q)
        keep(state, *traces_of(state))
        return carry

    lax.fori_loop(0, SECTIONS - 1, section, 0)
    local_part(RK_A[-1], RK_B[-1])
    sent(SECTIONS - 1)
    arrive(SECTIONS - 1)
    far_part(SECTIONS - 1, RK_B[-1], last=True)


def hand_on(x_ref, out_ref, sem):
    copy = pltpu.make_async_copy(x_ref, out_ref, sem)
    copy.start()
    copy.wait()


def shards(n_group, n_sub, fields, diff_ops, face_interp, *rest):
    rows = jnp.transpose(fields, (1, 0, 2)).reshape(4 * NP, ELEM)
    args = (rows, diff_ops, jnp.transpose(face_interp, (1, 0))) + rest
    vm = pltpu.VMEM
    loaded = [
        pltpu.SMEM(x.shape, x.dtype) if i == 7 else vm(x.shape, x.dtype) for i, x in enumerate(args)
    ]
    args = tuple(pltpu.with_memory_space_constraint(x, pltpu.HBM) for x in args)
    out = pl.pallas_call(
        functools.partial(kernel, n_group, n_sub),
        out_shape=jax.ShapeDtypeStruct(rows.shape, F32),
        in_specs=[pl.BlockSpec(memory_space=pl.ANY)] * len(args),
        out_specs=pl.BlockSpec(memory_space=pltpu.VMEM),
        scratch_shapes=loaded
        + [
            vm((4, NR, ELEM), F32),
            vm((4, NR, ELEM), F32),
            vm((256, FACES), BF16),
            vm((4 * FR, NP), F32),
            vm((4 * FR, 256), BF16),
            vm((3, NR, 256), BF16),
            vm((2 * NR, 256), BF16),
            vm((SLOTS, FACES), BF16),
            vm((FACES, FACES), BF16),
            vm((2 * SLOTS, FACES), BF16),
            vm((5, 4, 8, ELEM), F32),
            vm((3, 3, 8, ELEM), F32),
            vm((4 * FR, 3 * 4 * FR), BF16),
            vm((2 * SLOTS, ELEM), BF16),
            vm((2 * SLOTS, FACES), BF16),
            vm((4, 4, 8, ELEM), F32),
            vm((2, 4, 8, ELEM), F32),
            vm((4, 8, ELEM), F32),
            vm((SLOTS, 128), F32),
            vm((4, 4, FR, ELEM), F32),
            vm((256, FACES), BF16),
            vm((SECTIONS, 4, CAP, 128), F32),
            vm((SECTIONS, 4, CAP, 128), F32),
            pltpu.SemaphoreType.DMA((len(args),)),
            pltpu.SemaphoreType.DMA((4,)),
            pltpu.SemaphoreType.DMA((2, 4)),
        ],
        compiler_params=pltpu.CompilerParams(
            collective_id=0, has_side_effects=True, vmem_limit_bytes=16 << 20
        ),
        name="sections",
    )(*args)
    out = pl.pallas_call(
        hand_on,
        out_shape=jax.ShapeDtypeStruct(out.shape, F32),
        in_specs=[pl.BlockSpec(memory_space=pltpu.VMEM)],
        out_specs=pl.BlockSpec(memory_space=pl.ANY),
        scratch_shapes=[pltpu.SemaphoreType.DMA],
        compiler_params=pltpu.CompilerParams(vmem_limit_bytes=8 << 20),
        name="hand_on",
    )(out)
    return jnp.transpose(out.reshape(NP, 4, ELEM), (1, 0, 2))


def solution(mesh):
    both = ("group", "sub")
    return jax.shard_map(
        functools.partial(shards, mesh.shape["group"], mesh.shape["sub"]),
        mesh=mesh,
        in_specs=(
            P(None, None, both),
            P(),
            P(),
            P(),
            P(None, None, both),
            P(None, both),
            P(None, None, both),
            P(),
            P(None, both),
            P(None, both),
            P(None, both),
        ),
        out_specs=P(None, None, both),
        check_vma=False,
    )
```
